128 devices in a mesh: ctx: 16 (over z_lo, y, core), head: 8 (over x, z_hi).
Axes of the slice: x: 4, y: 4, z: 4 (z_hi: 2, z_lo: 2; z = z_hi * 2 + z_lo), core: 2. Of those that a mesh axis runs over, the one named last changes fastest.
Arguments:
- q_in: bfloat16 [12288, 4096], P('ctx', 'head'), may hold values from -6 to 6
- k_in: bfloat16 [12288, 4096], P('ctx', 'head'), may hold values from -6 to 6
- v_in: bfloat16 [12288, 4096], P('ctx', 'head'), may hold values from -6 to 6
- log_decay: float32 [12288, 32], P('ctx', 'head'), may hold values from -1 to 0, as said below
- block_doc: int32 [48], P('ctx'), may hold values from 0 to 2, as said below
- w_out: bfloat16 [4096, 6144], P('head'), may hold values from -0.09375 to 0.09375
- grad_y: bfloat16 [12288, 6144], P('ctx'), may hold values from -6 to 6
Outputs:
- out_y: bfloat16 [12288, 6144], P('ctx', 'head')
- grad_q: bfloat16 [12288, 4096], P('ctx', 'head')
- grad_k: bfloat16 [12288, 4096], P('ctx', 'head')
- grad_v: bfloat16 [12288, 4096], P('ctx', 'head')
- grad_w: bfloat16 [4096, 6144], P('head', 'ctx')
The draws below stay inside these ranges and needn't reach their ends.
Inputs may be any that keep to these rules, and one draw needn't show every extreme that they name: `log_decay`: every entry is negative. `block_doc`: block 0 has id 0, and the id of each later block equals that of the block before it or exceeds it by one; the sequence holds exactly 3 documents.
All inputs are finite; a program needn't handle non-finite values.
Results may differ from the reference program's by a relative error of at most 0.027.
Values may be sent and summed in bfloat16 or wider, within the bound.
A program may use at most 128 MiB of HBM per device.

```python
import math
import jax
import jax.numpy as jnp
from jax import lax

D = 6144
HEADS = 32
DH = 128
BL = 256
TOK_DEV = 768
SEQUENCE_TOKENS = 12288
NB = 48
HD = 4096
N_CTX = 16
N_HEAD = 8


def draw_log_decay(key, part):
    key_rows = jax.random.split(key, 7)
    fast_share = 0.5
    pick = jax.random.uniform(key_rows[0], (HEADS,), jnp.float32)
    fast_rate = jnp.exp(jax.random.uniform(key_rows[1], (HEADS,), jnp.float32, math.log(1.0 / 50.0), math.log(1.0 / 30.0)))
    slow_rate = jnp.exp(jax.random.uniform(key_rows[2], (HEADS,), jnp.float32, math.log(0.05), math.log(0.5))) / SEQUENCE_TOKENS
    decay_rate = jnp.where(pick < fast_share, fast_rate, slow_rate)
    range_decay_factor = jnp.exp(jax.random.uniform(key_rows[3], (SEQUENCE_TOKENS // TOK_DEV, 1), jnp.float32, math.log(0.5), math.log(2.0)))
    range_decay_factor = jnp.repeat(range_decay_factor, TOK_DEV, axis=0)
    token_decay_factor = jnp.exp(jax.random.uniform(key_rows[4], (SEQUENCE_TOKENS, HEADS), jnp.float32, math.log(0.5), math.log(2.0)))
    random_draw_pick = jax.random.uniform(key_rows[5], (SEQUENCE_TOKENS, 1), jnp.float32)
    random_loss_draws = jnp.log(jax.random.uniform(key_rows[6], (SEQUENCE_TOKENS, 1), jnp.float32, 0.5, 0.8))
    random_draws = jnp.where(random_draw_pick < 3.0 / SEQUENCE_TOKENS, random_loss_draws, 0.0)
    return (-decay_rate[None, :] * range_decay_factor * token_decay_factor + random_draws).astype(jnp.float32)


def draw_block_doc(key, part):
    doc_count = max(NB // 16, 2)
    order = jax.random.permutation(key, NB - 1) + 1
    chosen = order[:doc_count - 1]
    flags = jnp.any(jnp.arange(NB)[:, None] == chosen[None, :], axis=1).astype(jnp.int32)
    return jnp.cumsum(flags).astype(jnp.int32)


def raised(result, rng, source, target, shards_of, factor):
    def block_of(axis_at):
        return (jnp.arange(result.shape[axis_at]) // (result.shape[axis_at] // shards_of)).reshape((-1,) + (1,) * (result.ndim - 1 - axis_at))

    first = jax.random.permutation(rng, shards_of)[block_of(target)]
    second = (block_of(target) + shards_of // 2) % shards_of
    return jnp.where((block_of(source) == first) | (block_of(source) == second), factor * result, result)


def level_of(stream_key, extent, cuts, smallest, high):
    gain = 1.0
    for axis_at, blocks in cuts:
        heights = jax.random.uniform(jax.random.fold_in(jax.random.fold_in(stream_key, 6), axis_at), (blocks,), jnp.float32, smallest / len(cuts), high / len(cuts))
        gain = gain * jnp.repeat(jnp.exp(heights), extent[axis_at] // blocks).reshape((-1,) + (1,) * (len(extent) - 1 - axis_at))
    return gain


def bell_draw(rng, shape, scale, reach, cuts=(), kind=jnp.bfloat16):
    factor_of = level_of(rng, shape, cuts, -0.22, 0.18) if cuts else 1.0
    result = jax.random.normal(rng, shape, jnp.float32) * scale * factor_of
    return jnp.minimum(jnp.maximum(result, -reach), reach).astype(kind)


def heavy_noise(own_key, shape, scale, bound, cuts, heavy, dtype=jnp.bfloat16):
    result = scale * jax.random.normal(own_key, shape, jnp.float32)
    if cuts:
        result = result * level_of(own_key, shape, cuts, -0.22, 0.18)
    return jnp.clip(raised(result, jax.random.fold_in(own_key, 3), *heavy), -bound, bound).astype(dtype)


def setup_inputs(seed: int = 0) -> dict:
    splits = jax.random.split(jax.random.key(seed), 8)
    q_in = bell_draw(splits[0], (SEQUENCE_TOKENS, HD), 1.0, 6.0, ((0, 16), (1, 8)))
    k_in = bell_draw(splits[1], (SEQUENCE_TOKENS, HD), 1.0, 6.0, ((0, 16), (1, 8)))
    v_in = bell_draw(splits[2], (SEQUENCE_TOKENS, HD), 1.0, 6.0, ((0, 16), (1, 8)))
    log_decay = draw_log_decay(jax.random.fold_in(splits[7], 71), 0)
    block_doc = draw_block_doc(jax.random.fold_in(splits[7], 71), 0)
    w_out = bell_draw(splits[5], (HD, D), HD ** -0.5, 0.09375, ((0, 8),))
    grad_y = heavy_noise(splits[6], (SEQUENCE_TOKENS, D), 1.0, 6.0, ((0, 16),), (0, 1, 16, 2.0))
    return {"q_in": q_in, "k_in": k_in, "v_in": v_in, "log_decay": log_decay, "block_doc": block_doc, "w_out": w_out, "grad_y": grad_y}


def block_mask(decay_block):
    heads_first = jnp.swapaxes(decay_block, -1, -2)
    gap = heads_first[..., :, None] - heads_first[..., None, :]
    lower = jnp.arange(BL)[:, None] >= jnp.arange(BL)[None, :]
    return jnp.where(lower, jnp.exp(jnp.minimum(gap, 0.0)), 0.0)

def forward_block(pieces):
    q_block, k_block, v_block, decay_block, state_block = pieces
    mask = block_mask(decay_block)
    scores = jnp.einsum('ihd,jhd->hij', q_block.astype(jnp.float32), k_block.astype(jnp.float32))
    probs = (scores * mask).astype(jnp.bfloat16)
    intra = jnp.einsum('hij,jhd->ihd', probs.astype(jnp.float32), v_block.astype(jnp.float32))
    inter = jnp.einsum('ihd,hde->ihe', q_block.astype(jnp.float32), state_block.astype(jnp.float32))
    return intra + jnp.exp(decay_block)[..., None] * inter

def backward_block(pieces):
    q_block, k_block, v_block, decay_block, state_block, grad_block, egrad_block, kw_block = pieces
    mask = block_mask(decay_block)
    scores = jnp.einsum('ihd,jhd->hij', q_block.astype(jnp.float32), k_block.astype(jnp.float32))
    probs = (scores * mask).astype(jnp.bfloat16)
    dscore = (jnp.einsum('ihd,jhd->hij', grad_block.astype(jnp.float32), v_block.astype(jnp.float32)) * mask).astype(jnp.bfloat16)
    head_decay = jnp.exp(decay_block)
    tail_decay = jnp.exp(decay_block[-1:] - decay_block)
    grad_query = jnp.einsum('hij,jhd->ihd', dscore.astype(jnp.float32), k_block.astype(jnp.float32))
    grad_query = grad_query + head_decay[..., None] * jnp.einsum('ihe,hde->ihd', grad_block.astype(jnp.float32), state_block.astype(jnp.float32))
    grad_key = jnp.einsum('hij,ihd->jhd', dscore.astype(jnp.float32), q_block.astype(jnp.float32))
    grad_key = grad_key + tail_decay[..., None] * jnp.einsum('jhe,hde->jhd', v_block.astype(jnp.float32), egrad_block.astype(jnp.float32))
    grad_value = jnp.einsum('hij,ihd->jhd', probs.astype(jnp.float32), grad_block.astype(jnp.float32))
    grad_value = grad_value + jnp.einsum('jhd,hde->jhe', kw_block.astype(jnp.float32), egrad_block.astype(jnp.float32))
    return (grad_query.astype(jnp.bfloat16), grad_key.astype(jnp.bfloat16), grad_value.astype(jnp.bfloat16))

def reference(q_in, k_in, v_in, log_decay, block_doc, w_out, grad_y):
    nblocks = SEQUENCE_TOKENS // BL
    q_blocks = q_in.reshape(nblocks, BL, HEADS, DH)
    k_blocks = k_in.reshape(nblocks, BL, HEADS, DH)
    v_blocks = v_in.reshape(nblocks, BL, HEADS, DH)
    decay_sum = jnp.cumsum(log_decay.reshape(nblocks, BL, HEADS), axis=1)
    block_decay = jnp.exp(decay_sum[:, -1, :])
    tail_decay = jnp.exp(decay_sum[:, -1:, :] - decay_sum)
    head_decay = jnp.exp(decay_sum)
    k_weighted = (k_blocks.astype(jnp.float32) * tail_decay[..., None]).astype(jnp.bfloat16)
    block_state = jnp.einsum('nthd,nthe->nhde', k_weighted.astype(jnp.float32), v_blocks.astype(jnp.float32))
    same_doc = (block_doc[1:] == block_doc[:-1]).astype(jnp.float32)
    keep = jnp.concatenate([jnp.zeros((1,), jnp.float32), same_doc])
    keep_next = jnp.concatenate([same_doc, jnp.zeros((1,), jnp.float32)])
    zero_state = jnp.zeros((HEADS, DH, DH), jnp.float32)

    def forward_step(state, items):
        decay_here, update, keep_here = items
        return (keep_here * (decay_here[:, None, None] * state + update), state)
    _, state_before = lax.scan(forward_step, zero_state, (block_decay, block_state, keep_next))
    state_half = state_before.astype(jnp.bfloat16)
    attended = lax.map(forward_block, (q_blocks, k_blocks, v_blocks, decay_sum, state_half))
    inv_rms = lax.rsqrt(lax.optimization_barrier(jnp.mean(attended * attended, axis=-1, keepdims=True)) + 1e-06)
    normed = (attended * inv_rms).astype(jnp.bfloat16).reshape(SEQUENCE_TOKENS, HEADS * DH)
    width = HEADS * DH // N_HEAD
    total = jnp.zeros((SEQUENCE_TOKENS, D), jnp.float32)
    for group in range(N_HEAD):
        partial_y = jnp.dot(normed[:, group * width:(group + 1) * width], w_out[group * width:(group + 1) * width], preferred_element_type=jnp.float32)
        total = total + lax.optimization_barrier(partial_y.astype(jnp.bfloat16)).astype(jnp.float32)
    out_y = total.astype(jnp.bfloat16)
    grad_normed = lax.dot_general(grad_y, w_out, (((1,), (1,)), ((), ())), preferred_element_type=jnp.float32)
    grad_normed = grad_normed.reshape(nblocks, BL, HEADS, DH)
    inner = lax.optimization_barrier(jnp.mean(grad_normed * attended, axis=-1, keepdims=True))
    grad_attn = (inv_rms * (grad_normed - attended * (inv_rms * inv_rms) * inner)).astype(jnp.bfloat16)
    q_weighted = (q_blocks.astype(jnp.float32) * head_decay[..., None]).astype(jnp.bfloat16)
    direct = jnp.einsum('nthd,nthe->nhde', q_weighted.astype(jnp.float32), grad_attn.astype(jnp.float32))

    def backward_step(egrad, items):
        direct_here, decay_here, keep_here = items
        return (keep_here * (direct_here + decay_here[:, None, None] * egrad), egrad)
    _, state_grad = lax.scan(backward_step, zero_state, (direct, block_decay, keep), reverse=True)
    state_grad_half = state_grad.astype(jnp.bfloat16)
    grad_q, grad_k, grad_v = lax.map(backward_block, (q_blocks, k_blocks, v_blocks, decay_sum, state_half, grad_attn, state_grad_half, k_weighted))
    weight_total = jnp.zeros((HEADS * DH, D), jnp.float32)
    for group in range(N_CTX):
        rows_normed = normed[group * TOK_DEV:(group + 1) * TOK_DEV]
        rows_grad = grad_y[group * TOK_DEV:(group + 1) * TOK_DEV]
        partial_w = lax.dot_general(rows_normed, rows_grad, (((0,), (0,)), ((), ())), preferred_element_type=jnp.float32)
        weight_total = weight_total + lax.optimization_barrier(partial_w.astype(jnp.bfloat16)).astype(jnp.float32)
    grad_w = weight_total.astype(jnp.bfloat16)
    return (out_y, grad_q.reshape(SEQUENCE_TOKENS, HEADS * DH), grad_k.reshape(SEQUENCE_TOKENS, HEADS * DH), grad_v.reshape(SEQUENCE_TOKENS, HEADS * DH), grad_w)
```

```python
import functools

import jax
import jax.numpy as jnp
from jax import lax
from jax.experimental import pallas as pl
from jax.experimental.pallas import tpu as pltpu
from jax.sharding import PartitionSpec as P

DH = 128
BL = 256
EPS = 1e-06
F32 = jnp.float32
BF16 = jnp.bfloat16
MESH = pl.DeviceIdType.MESH

N_CTX = 16
N_HEAD = 8
N_CHIP = 8
NBLK = 3
HEADS = 4
TOK = NBLK * BL
HALF = TOK // 2
FEAT = HEADS * DH
D = 6144
COLS_Y = D // N_HEAD
COLS_W = D // N_CTX
W_ROWS = FEAT // N_CTX

NN = (((1,), (0,)), ((), ()))
NT = (((1,), (1,)), ((), ()))
TN = (((0,), (0,)), ((), ()))


def mm(a, b, dims=NN):
    return lax.dot_general(a, b, dims, preferred_element_type=F32)


def kernel(
    q, k, v, ld, ldt, scal, w_hbm, gy_hbm,
    out_y, gq, gk, gv, gw,
    w, gy, dsc, dsr, run, loc, sth, gloc, sgh, pr, att, gn, inv_s, ga, n_t,
    nall, wcol, crx, rs_rx, sbuf, gbuf, st_rx, gr_rx, scal_rx, wgt, entry, acc,
    lsem, wa_s, wa_r, wg_s, wg_r, wf_s, sc_s, sc_r, st_s, st_r, gr_s, gr_r,
    ag_s, ag_r, cs_s, cs_r, ps_s, ps_r,
):
    c = lax.axis_index("ctx")
    h = lax.axis_index("head")
    chip, core = c // 2, lax.rem(c, 2)
    partner = c + 1 - 2 * core
    hx, hz = h // 2, lax.rem(h, 2)
    east = lax.rem(hx + 1, 4) * 2 + hz
    west = lax.rem(hx + 3, 4) * 2 + hz
    zp = hx * 2 + 1 - hz
    east_z = lax.rem(hx + 1, 4) * 2 + 1 - hz
    west_z = lax.rem(hx + 3, 4) * 2 + 1 - hz
    far = lax.rem(hx + 2, 4) * 2 + hz
    far_z = lax.rem(hx + 2, 4) * 2 + 1 - hz

    def remote(src, dst, ssem, rsem, to_c, to_h):
        return pltpu.make_async_remote_copy(
            src_ref=src, dst_ref=dst, send_sem=ssem, recv_sem=rsem,
            device_id=(to_c, to_h), device_id_type=MESH,
        )

    load_w = pltpu.make_async_copy(w_hbm, w, lsem.at[0])
    load_g = pltpu.make_async_copy(gy_hbm, gy, lsem.at[1])

    def w_piece(to):
        return w_hbm.at[pl.ds(pl.multiple_of(c * W_ROWS, W_ROWS), W_ROWS),
                        pl.ds(pl.multiple_of(to * COLS_Y, COLS_Y), COLS_Y)]

    own_w = pltpu.make_async_copy(w_piece(h), wcol.at[h, c], lsem.at[2])
    own_w.start()

    barrier = pltpu.get_barrier_semaphore()
    for d in range(1, N_CTX):
        pl.semaphore_signal(barrier, inc=1, device_id=(lax.rem(c + d, N_CTX), h),
                            device_id_type=MESH)
    for d in range(1, N_HEAD):
        pl.semaphore_signal(barrier, inc=1, device_id=(c, lax.rem(h + d, N_HEAD)),
                            device_id_type=MESH)
    pl.semaphore_wait(barrier, N_CTX + N_HEAD - 2)

    def w_spread(d):
        to = lax.rem(h + d, N_HEAD)
        return remote(w_piece(to), wcol.at[h, c], wa_s.at[d], wa_r.at[h], c, to)

    def scal_spread(d):
        return remote(scal, scal_rx.at[c], sc_s.at[d], sc_r.at[c], lax.rem(c + d, N_CTX), h)

    for d in range(1, N_HEAD):
        w_spread(d).start()
    for d in range(1, N_CTX):
        scal_spread(d).start()
    load_w.start()
    load_g.start()
    scal_rx[c] = scal[...]

    at_row = lax.broadcasted_iota(jnp.int32, (BL, BL), 0)
    at_col = lax.broadcasted_iota(jnp.int32, (BL, BL), 1)
    lower = at_row >= at_col

    first, mid, last = scal[4:5, 0:1], scal[6:7, 0:1], scal[5:6, 0:1]
    keep1 = jnp.where(first == mid, 1.0, 0.0)
    keep2 = jnp.where(mid == last, 1.0, 0.0)

    def rows_of(b):
        return pl.ds(pl.multiple_of(b * BL, BL), BL)

    def cols_of(hh):
        return slice(hh * DH, (hh + 1) * DH)

    def mask_of(rows, hh):
        gap = dsc[rows, hh:hh + 1] - dsr[hh:hh + 1, rows]
        return jnp.where(lower, jnp.exp(jnp.minimum(gap, 0.0)), 0.0)

    def pick(b, zero, one, two):
        return jnp.where(b == 0, zero, jnp.where(b == 1, one, two))

    run[...] = jnp.zeros_like(run)

    def local_states(b, carry):
        rows = rows_of(b)
        tri = jnp.where(lower, 1.0, 0.0).astype(F32)
        dsc[rows, :] = jnp.dot(tri, ld[rows, :], precision=lax.Precision.HIGHEST,
                               preferred_element_type=F32)
        dsr[:, rows] = lax.dot_general(ldt[:, rows], tri, NT, precision=lax.Precision.HIGHEST,
                                       preferred_element_type=F32)
        kept = pick(b, keep1, keep2, jnp.ones_like(keep1))
        for hh in range(HEADS):
            col = dsc[rows, hh:hh + 1]
            end = col[BL - 1:BL, :]
            kw = (k[rows, cols_of(hh)].astype(F32) * jnp.exp(end - col)).astype(BF16)
            update = mm(kw, v[rows, cols_of(hh)], TN)
            loc[b, hh] = run[hh]
            run[hh] = kept * (jnp.exp(end) * run[hh] + update)
        return carry

    lax.fori_loop(0, NBLK, local_states, 0)
    for hh in range(HEADS):
        sbuf[cols_of(hh), :] = run[hh].astype(BF16)

    def state_send(d):
        return remote(sbuf, st_rx.at[c], st_s.at[d], st_r.at[c], c + d, h)

    for d in range(1, N_CTX):
        @pl.when(c + d < N_CTX)
        def _():
            state_send(d).start()

    own_w.wait()
    for d in range(1, N_HEAD):
        src = lax.rem(h + d, N_HEAD)
        remote(w_piece(h), wcol.at[src, c], wa_s.at[d], wa_r.at[src], c, src).wait_recv()

    def w_gather(d):
        to = lax.rem(chip + d, N_CHIP) * 2 + core
        return remote(wcol.at[:, c], wcol.at[:, c], wg_s.at[d], wg_r.at[c], to, h)

    w_partner = remote(wcol.at[:, c], wcol.at[:, c], wg_s.at[0], wg_r.at[c], partner, h)
    w_partner.start()
    for d in range(1, N_CHIP):
        w_gather(d).start()

    def intra(b, carry):
        rows = rows_of(b)
        for hh in range(HEADS):
            cols = cols_of(hh)
            probs = (mm(q[rows, cols], k[rows, cols], NT) * mask_of(rows, hh)).astype(BF16)
            pr[b, hh] = probs
            att[rows, cols] = mm(probs, v[rows, cols])
        return carry

    lax.fori_loop(0, NBLK, intra, 0)

    load_w.wait()
    load_g.wait()
    gn[...] = jnp.zeros_like(gn)
    step_k = 1024

    def grad_normed(i, carry):
        at = pl.ds(pl.multiple_of(i * step_k, step_k), step_k)
        gn[...] += mm(gy[:, at], w[:, at], NT)
        return carry

    lax.fori_loop(0, D // step_k, grad_normed, 0)

    for d in range(1, N_CTX):
        src = lax.rem(c + d, N_CTX)
        remote(scal, scal_rx.at[src], sc_s.at[d], sc_r.at[src], src, h).wait_recv()

    def weights(reverse):
        total = jnp.zeros((8, DH), F32)
        order = range(N_CTX) if reverse else range(N_CTX - 1, -1, -1)
        for r in order:
            there = scal_rx[r]
            inside = (c < r) if reverse else (r < c)
            same = (there[4:5, :] == scal[5:6, :]) if reverse else (there[5:6, :] == scal[4:5, :])
            gate = jnp.where(same, 1.0, 0.0) * jnp.where(inside, 1.0, 0.0)
            wgt[r] = jnp.exp(total) * gate
            total = total + there * jnp.where(inside, 1.0, 0.0)

    def gather_states(reverse, rx, rsem, ssem, buf):
        weights(reverse)
        entry[...] = jnp.zeros_like(entry)

        def add(r, carry):
            @pl.when((r > c) if reverse else (r < c))
            def _():
                remote(buf, rx.at[r], ssem.at[0], rsem.at[r], r, h).wait_recv()
                for hh in range(HEADS):
                    entry[hh] += wgt[r, hh:hh + 1, :] * rx[r, cols_of(hh), :].astype(F32)
            return carry

        lax.fori_loop(0, N_CTX, add, 0)

    gather_states(False, st_rx, st_r, st_s, sbuf)

    def end_of(b, hh):
        return jnp.exp(dsc[b * BL + BL - 1:(b + 1) * BL, hh:hh + 1])

    def inter(b, carry):
        rows = rows_of(b)
        for hh in range(HEADS):
            cols = cols_of(hh)
            coef1 = keep1 * end_of(0, hh)
            coef = pick(b, jnp.ones_like(keep1), coef1, keep2 * end_of(1, hh) * coef1)
            state = (loc[b, hh] + coef * entry[hh]).astype(BF16)
            sth[b, hh] = state
            a = att[rows, cols] + jnp.exp(dsc[rows, hh:hh + 1]) * mm(q[rows, cols], state)
            inv = lax.rsqrt(jnp.mean(a * a, axis=-1, keepdims=True) + EPS)
            n = a * inv
            att[rows, cols] = a
            inv_s[rows, hh:hh + 1] = inv
            nall[h, rows, cols] = n.astype(BF16)
            n_t[cols, rows] = n.T.astype(BF16)
        return carry

    lax.fori_loop(0, NBLK, inter, 0)

    def part(slot, half):
        return nall.at[slot, pl.ds(half * HALF, HALF), :]

    def hand(slot, half, sem, to):
        return remote(part(slot, half), part(slot, half), ag_s.at[sem], ag_r.at[slot, half], c, to)

    def arrive(slot, half):
        remote(part(slot, half), part(slot, half), ag_s.at[0], ag_r.at[slot, half], c, zp).wait_recv()

    sent = []

    def go(*args):
        copy = hand(*args)
        copy.start()
        sent.append(copy)

    for half in range(2):
        go(h, half, half, zp)
        go(h, half, 2 + half, east)
        go(h, half, 4 + half, west)

    run[...] = jnp.zeros_like(run)

    def local_grads(i, carry):
        b = NBLK - 1 - i
        rows = rows_of(b)
        kept = pick(b, jnp.ones_like(keep1), keep1, keep2)
        for hh in range(HEADS):
            cols = cols_of(hh)
            a, g, inv = att[rows, cols], gn[rows, cols], inv_s[rows, hh:hh + 1]
            mean = jnp.mean(g * a, axis=-1, keepdims=True)
            grad = (inv * (g - a * (inv * inv) * mean)).astype(BF16)
            ga[rows, cols] = grad
            col = dsc[rows, hh:hh + 1]
            qw = (q[rows, cols].astype(F32) * jnp.exp(col)).astype(BF16)
            direct = mm(qw, grad, TN)
            gloc[b, hh] = run[hh]
            run[hh] = kept * (direct + jnp.exp(col[BL - 1:BL, :]) * run[hh])
        return carry

    lax.fori_loop(0, NBLK, local_grads, 0)
    for hh in range(HEADS):
        gbuf[cols_of(hh), :] = run[hh].astype(BF16)

    def grad_send(d):
        return remote(gbuf, gr_rx.at[c], gr_s.at[d], gr_r.at[c], c - d, h)

    for d in range(1, N_CTX):
        @pl.when(c >= d)
        def _():
            grad_send(d).start()

    def w_cols(i, parity):
        return pl.ds(pl.multiple_of((2 * i + parity) * COLS_W, COLS_W), COLS_W)

    def to_partner(i):
        return remote(w.at[:, w_cols(i, 1 - core)], crx.at[i], cs_s.at[i], cs_r.at[i], partner, h)

    def from_partner(i):
        return remote(w.at[:, w_cols(i, core)], crx.at[i], cs_s.at[i], cs_r.at[i], partner, h)

    def to_owner(i):
        return remote(w.at[:, w_cols(i, core)], rs_rx.at[chip], ps_s.at[i], ps_r.at[chip],
                      2 * i + core, h)

    def other_columns(j, carry):
        i = lax.rem(chip + 1 + j, N_CHIP)
        at = w_cols(i, 1 - core)
        w[:, at] = mm(n_t[...], gy[:, at]).astype(BF16)
        to_partner(i).start()
        return carry

    lax.fori_loop(0, N_CHIP, other_columns, 0)

    def own_columns(j, carry):
        i = lax.rem(chip + 1 + j, N_CHIP)
        at = w_cols(i, core)
        product = mm(n_t[...], gy[:, at])
        from_partner(i).wait_recv()
        both = (product + crx[i].astype(F32)).astype(BF16)

        @pl.when(j < N_CHIP - 1)
        def _():
            w[:, at] = both
            to_owner(i).start()

        @pl.when(j == N_CHIP - 1)
        def _():
            rs_rx[chip] = both
        return carry

    lax.fori_loop(0, N_CHIP, own_columns, 0)

    arrive(west, 0)
    go(west, 0, 6, east)
    arrive(east, 1)
    go(east, 1, 7, west)

    gather_states(True, gr_rx, gr_r, gr_s, gbuf)

    def backward(b, carry):
        rows = rows_of(b)
        for hh in range(HEADS):
            cols = cols_of(hh)
            coef1 = keep2 * end_of(2, hh)
            coef = pick(b, keep1 * end_of(1, hh) * coef1, coef1, jnp.ones_like(keep1))
            sg = (gloc[b, hh] + coef * entry[hh]).astype(BF16)
            qb, kb, vb, gb = q[rows, cols], k[rows, cols], v[rows, cols], ga[rows, cols]
            col = dsc[rows, hh:hh + 1]
            tail = jnp.exp(col[BL - 1:BL, :] - col)
            ds = (mm(gb, vb, NT) * mask_of(rows, hh)).astype(BF16)
            gq[rows, cols] = (mm(ds, kb) + jnp.exp(col) * mm(gb, sth[b, hh], NT)).astype(BF16)
            gk[rows, cols] = (mm(ds, qb, TN) + tail * mm(vb, sg, NT)).astype(BF16)
            kw = (kb.astype(F32) * tail).astype(BF16)
            gv[rows, cols] = (mm(pr[b, hh], gb, TN) + mm(kw, sg)).astype(BF16)
        return carry

    lax.fori_loop(0, NBLK, backward, 0)

    for half in range(2):
        arrive(zp, half)
        go(zp, half, 8 + half, east)
        go(zp, half, 10 + half, west)

    def w_forward(d):
        at = lax.rem(chip + d, N_CHIP) * 2 + core
        return remote(wcol.at[:, at], wcol.at[:, at], wf_s.at[d], wg_r.at[at], partner, h)

    def w_arrive(at):
        remote(wcol.at[:, at], wcol.at[:, at], wg_s.at[0], wg_r.at[at], partner, h).wait_recv()

    for d in range(1, N_CHIP):
        w_arrive(lax.rem(chip + d, N_CHIP) * 2 + core)
        w_forward(d).start()
    for d in range(N_CHIP):
        w_arrive(lax.rem(chip + d, N_CHIP) * 2 + 1 - core)

    def product(slot, start):
        def rows_step(b, carry):
            rows = rows_of(b)
            term = mm(nall[slot, rows, :], wcol[slot].reshape(FEAT, COLS_Y))
            if start:
                acc[rows, :] = term
            else:
                acc[rows, :] += term
            return carry

        lax.fori_loop(0, NBLK, rows_step, 0)

    product(h, True)
    arrive(west, 1)
    product(west, False)
    arrive(east, 0)
    product(east, False)
    product(zp, False)
    arrive(west_z, 0)
    go(west_z, 0, 12, east)
    arrive(east_z, 1)
    go(east_z, 1, 13, west)
    arrive(far, 0)
    arrive(far, 1)
    product(far, False)

    total = rs_rx[chip].astype(F32)
    for d in range(1, N_CHIP):
        src = lax.rem(chip + d, N_CHIP)
        remote(w.at[:, w_cols(src, core)], rs_rx.at[src], ps_s.at[src], ps_r.at[src],
               2 * src + core, h).wait_recv()
    for d in range(1, N_CHIP):
        total = total + rs_rx[lax.rem(chip + d, N_CHIP)].astype(F32)
    gw[...] = total.astype(BF16)

    arrive(west_z, 1)
    product(west_z, False)
    arrive(east_z, 0)
    product(east_z, False)
    arrive(far_z, 0)
    arrive(far_z, 1)
    product(far_z, False)
    out_y[...] = acc[...].astype(BF16)

    for d in range(1, N_HEAD):
        w_spread(d).wait_send()
    for d in range(1, N_CTX):
        scal_spread(d).wait_send()

        @pl.when(c + d < N_CTX)
        def _():
            state_send(d).wait_send()

        @pl.when(c >= d)
        def _():
            grad_send(d).wait_send()
    w_partner.wait_send()
    for d in range(1, N_CHIP):
        w_gather(d).wait_send()
        w_forward(d).wait_send()
        to_owner(lax.rem(chip + d, N_CHIP)).wait_send()
    for i in range(N_CHIP):
        to_partner(i).wait_send()
    for copy in sent:
        copy.wait_send()


def per_device(q_in, k_in, v_in, log_decay, block_doc, w_out, grad_y):
    doc = block_doc.astype(F32)
    small = jnp.concatenate([
        jnp.sum(log_decay, axis=0), doc[:1], doc[-1:], doc[1:2], jnp.zeros((1,), F32)])
    scal = jnp.broadcast_to(small[:, None], (8, DH))
    ldt = jnp.pad(log_decay.T, ((0, 8 - HEADS), (0, 0)))
    vmem = pl.BlockSpec(memory_space=pltpu.VMEM)
    hbm = pl.BlockSpec(memory_space=pl.ANY)
    dma = pltpu.SemaphoreType.DMA
    head_shape = jax.ShapeDtypeStruct((TOK, FEAT), BF16)
    return pl.pallas_call(
        kernel,
        out_shape=(
            jax.ShapeDtypeStruct((TOK, COLS_Y), BF16),
            head_shape, head_shape, head_shape,
            jax.ShapeDtypeStruct((FEAT, COLS_W), BF16),
        ),
        in_specs=[vmem] * 6 + [hbm] * 2,
        out_specs=(vmem,) * 5,
        scratch_shapes=[
            pltpu.VMEM((FEAT, D), BF16),
            pltpu.VMEM((TOK, D), BF16),
            pltpu.VMEM((TOK, HEADS), F32),
            pltpu.VMEM((8, TOK), F32),
            pltpu.VMEM((HEADS, DH, DH), F32),
            pltpu.VMEM((NBLK, HEADS, DH, DH), F32),
            pltpu.VMEM((NBLK, HEADS, DH, DH), BF16),
            pltpu.VMEM((NBLK, HEADS, DH, DH), F32),
            pltpu.VMEM((8, DH), BF16),
            pltpu.VMEM((NBLK, HEADS, BL, BL), BF16),
            pltpu.VMEM((TOK, FEAT), F32),
            pltpu.VMEM((TOK, FEAT), F32),
            pltpu.VMEM((TOK, HEADS), F32),
            pltpu.VMEM((TOK, FEAT), BF16),
            pltpu.VMEM((FEAT, TOK), BF16),
            pltpu.VMEM((N_HEAD, TOK, FEAT), BF16),
            pltpu.VMEM((N_HEAD, N_CTX, W_ROWS, COLS_Y), BF16),
            pltpu.VMEM((N_CHIP, FEAT, COLS_W), BF16),
            pltpu.VMEM((N_CHIP, FEAT, COLS_W), BF16),
            pltpu.VMEM((FEAT, DH), BF16),
            pltpu.VMEM((FEAT, DH), BF16),
            pltpu.VMEM((N_CTX, FEAT, DH), BF16),
            pltpu.VMEM((N_CTX, FEAT, DH), BF16),
            pltpu.VMEM((N_CTX, 8, DH), F32),
            pltpu.VMEM((N_CTX, 8, DH), F32),
            pltpu.VMEM((HEADS, DH, DH), F32),
            pltpu.VMEM((TOK, COLS_Y), F32),
            dma((3,)),
            dma((N_HEAD,)), dma((N_HEAD,)),
            dma((N_CHIP,)), dma((N_CTX,)), dma((N_CHIP,)),
            dma((N_CTX,)), dma((N_CTX,)),
            dma((N_CTX,)), dma((N_CTX,)),
            dma((N_CTX,)), dma((N_CTX,)),
            dma((14,)), dma((N_HEAD, 2)),
            dma((N_CHIP,)), dma((N_CHIP,)),
            dma((N_CHIP,)), dma((N_CHIP,)),
        ],
        compiler_params=pltpu.CompilerParams(
            collective_id=0, has_side_effects=True, vmem_limit_bytes=62 << 20),
        name="attention_and_projection",
    )(q_in, k_in, v_in, log_decay, ldt, scal, w_out, grad_y)


def solution(mesh):
    in_specs = (
        P("ctx", "head"),
        P("ctx", "head"),
        P("ctx", "head"),
        P("ctx", "head"),
        P("ctx"),
        P("head", None),
        P("ctx", None),
    )
    out_specs = (
        P("ctx", "head"),
        P("ctx", "head"),
        P("ctx", "head"),
        P("ctx", "head"),
        P("head", "ctx"),
    )
    return jax.shard_map(
        per_device, mesh=mesh, in_specs=in_specs, out_specs=out_specs, check_vma=False
    )
```

```python
import jax
import jax.numpy as jnp
from jax import lax
from jax.experimental import pallas as pl
from jax.experimental.pallas import tpu as pltpu
from jax.sharding import PartitionSpec as P

DH = 128
BL = 256
EPS = 1e-06
F32 = jnp.float32
BF16 = jnp.bfloat16
MESH = pl.DeviceIdType.MESH

N_CTX = 16
N_HEAD = 8
N_CHIP = 8
NBLK = 3
HEADS = 4
TOK = NBLK * BL
HALF = TOK // 2
FEAT = HEADS * DH
D = 6144
COLS_Y = D // N_HEAD
COLS_W = D // N_CTX
W_PARTS = 4
W_ROWS = FEAT // W_PARTS

NN = (((1,), (0,)), ((), ()))
NT = (((1,), (1,)), ((), ()))
TN = (((0,), (0,)), ((), ()))


def mm(a, b, dims=NN):
    return lax.dot_general(a, b, dims, preferred_element_type=F32)


def kernel(
    docs, ldt, q_hbm, k_hbm, v_hbm, w_hbm, gy_hbm,
    out_y_hbm, gq_hbm, gk_hbm, gv_hbm, gw_hbm,
    q, k, v, w, gy, gq, gk, gv, gw, out_y,
    scal, dsc, dsr, run, loc, sth, gloc, pr, att, gn, inv_s, ga, n_t,
    nall, wcol, crx, rs_rx, z_rx, sbuf, p_rx, cbuf, c_rx, ebuf, e_rx, scal_rx, wgt, entry, acc,
    lsem, osem, wa_s, wa_r, wg_s, wg_r, sc_s, sc_r, x_s, x_r, st_s, st_r,
    ag_s, ag_r, cs_s, cs_r, ps_s, ps_r, z_s, z_r,
):
    c = lax.axis_index("ctx")
    h = lax.axis_index("head")
    chip, core = c // 2, lax.rem(c, 2)
    partner = c + 1 - 2 * core
    zl, y = c // 8, lax.rem(chip, 4)
    y_up = zl * 8 + lax.rem(y + 1, 4) * 2 + core
    y_down = zl * 8 + lax.rem(y + 3, 4) * 2 + core
    z_peer = lax.rem(c + 8, N_CTX)
    own_part = lax.rem(y, 2) * 2 + core
    far_part = (1 - lax.rem(y, 2)) * 2 + core
    hx, hz = h // 2, lax.rem(h, 2)
    east = lax.rem(hx + 1, 4) * 2 + hz
    west = lax.rem(hx + 3, 4) * 2 + hz
    zp = hx * 2 + 1 - hz
    east_z = lax.rem(hx + 1, 4) * 2 + 1 - hz
    west_z = lax.rem(hx + 3, 4) * 2 + 1 - hz
    far = lax.rem(hx + 2, 4) * 2 + hz
    far_z = lax.rem(hx + 2, 4) * 2 + 1 - hz

    def remote(src, dst, ssem, rsem, to_c, to_h):
        return pltpu.make_async_remote_copy(
            src_ref=src, dst_ref=dst, send_sem=ssem, recv_sem=rsem,
            device_id=(to_c, to_h), device_id_type=MESH,
        )

    loads = [
        pltpu.make_async_copy(src, dst, lsem.at[i])
        for i, (src, dst) in enumerate(
            [(k_hbm, k), (v_hbm, v), (q_hbm, q), (w_hbm, w), (gy_hbm, gy)])
    ]

    def w_piece(to):
        return w_hbm.at[pl.ds(pl.multiple_of(own_part * W_ROWS, W_ROWS), W_ROWS),
                        pl.ds(pl.multiple_of(to * COLS_Y, COLS_Y), COLS_Y)]

    own_w = pltpu.make_async_copy(w_piece(h), wcol.at[h, own_part], lsem.at[5])
    for copy in loads[:3]:
        copy.start()

    barrier = pltpu.get_barrier_semaphore()
    for d in range(1, N_CTX):
        pl.semaphore_signal(barrier, inc=1, device_id=(lax.rem(c + d, N_CTX), h),
                            device_id_type=MESH)
    for d in range(1, N_HEAD):
        pl.semaphore_signal(barrier, inc=1, device_id=(c, lax.rem(h + d, N_HEAD)),
                            device_id_type=MESH)
    pl.semaphore_wait(barrier, N_CTX + N_HEAD - 2)

    def w_spread(d):
        to = lax.rem(h + d, N_HEAD)
        return remote(w_piece(to), wcol.at[h, own_part], wa_s.at[d], wa_r.at[h], c, to)

    def scal_spread(d):
        return remote(scal, scal_rx.at[c], sc_s.at[d], sc_r.at[c], lax.rem(c + d, N_CTX), h)

    for copy in loads[3:]:
        copy.start()
    own_w.start()
    for d in range(1, N_HEAD):
        w_spread(d).start()

    at_row = lax.broadcasted_iota(jnp.int32, (BL, BL), 0)
    at_col = lax.broadcasted_iota(jnp.int32, (BL, BL), 1)
    lower = at_row >= at_col

    def doc_row(b):
        return jnp.full((1, DH), docs[b], jnp.int32).astype(F32)

    keep1 = jnp.where(doc_row(0) == doc_row(1), 1.0, 0.0)
    keep2 = jnp.where(doc_row(1) == doc_row(2), 1.0, 0.0)

    def rows_of(b):
        return pl.ds(pl.multiple_of(b * BL, BL), BL)

    def cols_of(hh):
        return slice(hh * DH, (hh + 1) * DH)

    def mask_of(rows, hh):
        gap = dsc[rows, hh:hh + 1] - dsr[hh:hh + 1, rows]
        return jnp.where(lower, jnp.exp(jnp.minimum(gap, 0.0)), 0.0)

    def pick(b, zero, one, two):
        return jnp.where(b == 0, zero, jnp.where(b == 1, one, two))

    run[...] = jnp.zeros_like(run)

    tri = jnp.where(lower, 1.0, 0.0).astype(F32)
    exact = dict(precision=lax.Precision.HIGHEST, preferred_element_type=F32)

    def sums(b, carry):
        rows = rows_of(b)
        dsc[rows, :] = lax.dot_general(tri, ldt[:, rows], NT, **exact)
        dsr[:, rows] = lax.dot_general(ldt[:, rows], tri, NT, **exact)
        return carry

    lax.fori_loop(0, NBLK, sums, 0)
    ends = [dsr[:, (b + 1) * BL - 1:(b + 1) * BL] for b in range(NBLK)]
    scal[0:HEADS, :] = jnp.broadcast_to(ends[0] + ends[1] + ends[2], (HEADS, DH))
    for row, b in ((4, 0), (5, NBLK - 1), (6, 1), (7, 1)):
        scal[row:row + 1, :] = doc_row(b)
    for d in range(1, N_CTX):
        scal_spread(d).start()
    scal_rx[c] = scal[...]

    def local_states(b, carry):
        rows = rows_of(b)
        kept = pick(b, keep1, keep2, jnp.ones_like(keep1))
        for hh in range(HEADS):
            col = dsc[rows, hh:hh + 1]
            end = col[BL - 1:BL, :]
            kw = (k[rows, cols_of(hh)].astype(F32) * jnp.exp(end - col)).astype(BF16)
            update = mm(kw, v[rows, cols_of(hh)], TN)
            loc[b, hh] = run[hh]
            run[hh] = kept * (jnp.exp(end) * run[hh] + update)
        return carry

    loads[0].wait()
    loads[1].wait()
    lax.fori_loop(0, NBLK, local_states, 0)
    for hh in range(HEADS):
        sbuf[0, cols_of(hh), :] = run[hh].astype(BF16)

    def pair(way):
        return remote(sbuf.at[way], p_rx.at[way], x_s.at[way, 0], x_r.at[way, 0], partner, h)

    def pass_on(way, d):
        to = chip - d if way else chip + d
        return remote(cbuf.at[way], c_rx.at[way, chip], st_s.at[way, d], st_r.at[way, chip],
                      2 * to + core, h)

    def swap(way):
        return remote(ebuf.at[way], e_rx.at[way], x_s.at[way, 1], x_r.at[way, 1], partner, h)

    def inside(way, d):
        return (chip >= d) if way else (chip + d < N_CHIP)

    pair(0).start()

    def intra(b, carry):
        rows = rows_of(b)
        for hh in range(HEADS):
            cols = cols_of(hh)
            probs = (mm(q[rows, cols], k[rows, cols], NT) * mask_of(rows, hh)).astype(BF16)
            pr[b, hh] = probs
            att[rows, cols] = mm(probs, v[rows, cols])
        return carry

    loads[2].wait()
    lax.fori_loop(0, NBLK, intra, 0)

    for d in range(1, N_CTX):
        src = lax.rem(c + d, N_CTX)
        remote(scal, scal_rx.at[src], sc_s.at[d], sc_r.at[src], src, h).wait_recv()

    for way in range(2):
        total = jnp.zeros((8, DH), F32)
        mine = scal_rx[2 * chip + 1, 5:6, :] if way else scal_rx[2 * chip, 4:5, :]
        for r in range(N_CHIP) if way else range(N_CHIP - 1, -1, -1):
            theirs = scal_rx[2 * r, 4:5, :] if way else scal_rx[2 * r + 1, 5:6, :]
            here = jnp.where((r > chip) if way else (r < chip), 1.0, 0.0)
            wgt[way, r] = jnp.exp(total) * jnp.where(theirs == mine, here, 0.0)
            total = total + here * (scal_rx[2 * r] + scal_rx[2 * r + 1])

    one = jnp.ones((8, DH), F32)

    def same(row, other):
        return jnp.where(scal_rx[2 * chip, row:row + 1, :] == scal_rx[2 * chip + 1, other:other + 1, :],
                         1.0, 0.0)

    log0, log1 = scal_rx[2 * chip], scal_rx[2 * chip + 1]
    from_core0 = jnp.exp(log1) * same(5, 5)
    from_core1 = jnp.exp(log0) * same(4, 4)
    through0 = jnp.exp(log0) * same(4, 4)
    through1 = jnp.exp(log1) * same(5, 5)
    link = same(5, 4) * one
    is0 = core == 0
    wgt[0, 8] = jnp.where(is0, from_core0, one)
    wgt[0, 9] = jnp.where(is0, one, from_core0)
    wgt[0, 10] = jnp.where(is0, one, through0)
    wgt[0, 11] = jnp.where(is0, 0.0, link)
    wgt[1, 8] = jnp.where(is0, one, from_core1)
    wgt[1, 9] = jnp.where(is0, from_core1, one)
    wgt[1, 10] = jnp.where(is0, through1, one)
    wgt[1, 11] = jnp.where(is0, link, 0.0)

    def head_rows(j):
        return pl.ds(pl.multiple_of((2 * core + j) * DH, DH), DH)

    def chip_state(way):
        pair(way).wait_recv()
        for j in range(2):
            hh = 2 * core + j
            cbuf[way, cols_of(j), :] = (
                wgt[way, 8, pl.ds(hh, 1), :] * run[hh]
                + wgt[way, 9, pl.ds(hh, 1), :] * p_rx[way, head_rows(j), :].astype(F32)
            ).astype(BF16)
        for d in range(1, N_CHIP):
            @pl.when(inside(way, d))
            def _():
                pass_on(way, d).start()

    def chip_entry(way):
        ebuf_f = entry
        for j in range(2):
            ebuf_f[j] = jnp.zeros((DH, DH), F32)

        def add(r, carry):
            @pl.when((r > chip) if way else (r < chip))
            def _():
                remote(cbuf.at[way], c_rx.at[way, r], st_s.at[way, 0], st_r.at[way, r],
                       2 * r + core, h).wait_recv()
                for j in range(2):
                    ebuf_f[j] += (wgt[way, r, pl.ds(2 * core + j, 1), :]
                                  * c_rx[way, r, cols_of(j), :].astype(F32))
            return carry

        lax.fori_loop(0, N_CHIP, add, 0)
        for j in range(2):
            ebuf[way, cols_of(j), :] = ebuf_f[j].astype(BF16)
        swap(way).start()

    def own_entry(way):
        swap(way).wait_recv()
        for j in range(2):
            for hh, chips in ((2 * core + j, ebuf), (2 * (1 - core) + j, e_rx)):
                rows = pl.ds(pl.multiple_of(hh * DH, DH), DH)
                entry[hh] = (wgt[way, 10, pl.ds(hh, 1), :] * chips[way, cols_of(j), :].astype(F32)
                             + wgt[way, 11, pl.ds(hh, 1), :] * p_rx[way, rows, :].astype(F32))

    chip_state(0)

    loads[3].wait()
    loads[4].wait()
    gn[...] = jnp.zeros_like(gn)
    step_k = 1024

    def grad_normed(i, carry):
        at = pl.ds(pl.multiple_of(i * step_k, step_k), step_k)
        gn[...] += mm(gy[:, at], w[:, at], NT)
        return carry

    lax.fori_loop(0, 4, grad_normed, 0)
    chip_entry(0)
    lax.fori_loop(4, D // step_k, grad_normed, 0)
    own_entry(0)

    def end_of(b, hh):
        return jnp.exp(dsc[b * BL + BL - 1:(b + 1) * BL, hh:hh + 1])

    def inter(b, carry):
        rows = rows_of(b)
        for hh in range(HEADS):
            cols = cols_of(hh)
            coef1 = keep1 * end_of(0, hh)
            coef = pick(b, jnp.ones_like(keep1), coef1, keep2 * end_of(1, hh) * coef1)
            state = (loc[b, hh] + coef * entry[hh]).astype(BF16)
            sth[b, hh] = state
            a = att[rows, cols] + jnp.exp(dsc[rows, hh:hh + 1]) * mm(q[rows, cols], state)
            inv = lax.rsqrt(jnp.mean(a * a, axis=-1, keepdims=True) + EPS)
            n = a * inv
            att[rows, cols] = a
            inv_s[rows, hh:hh + 1] = inv
            nall[h, rows, cols] = n.astype(BF16)
            n_t[cols, rows] = n.T.astype(BF16)
        return carry

    lax.fori_loop(0, NBLK, inter, 0)

    def part(slot, half):
        return nall.at[slot, pl.ds(half * HALF, HALF), :]

    def hand(slot, half, sem, to):
        return remote(part(slot, half), part(slot, half), ag_s.at[sem], ag_r.at[slot, half], c, to)

    def arrive(slot, half):
        remote(part(slot, half), part(slot, half), ag_s.at[0], ag_r.at[slot, half], c, zp).wait_recv()

    sent = []

    def go(*args):
        copy = hand(*args)
        copy.start()
        sent.append(copy)

    for half in range(2):
        go(h, half, half, zp)
        go(h, half, 2 + half, east)
        go(h, half, 4 + half, west)

    def w_cols(i, parity):
        return pl.ds(pl.multiple_of((2 * i + parity) * COLS_W, COLS_W), COLS_W)

    def to_partner(i):
        return remote(w.at[:, w_cols(i, 1 - core)], crx.at[i], cs_s.at[i], cs_r.at[i], partner, h)

    def from_partner(i):
        return remote(w.at[:, w_cols(i, core)], crx.at[i], cs_s.at[i], cs_r.at[i], partner, h)

    def order(j):
        return jnp.where(j < 4, 1 - zl, zl), lax.rem(y + 1 + lax.rem(j, 4), 4)

    def to_owner(layer, row):
        return remote(w.at[:, w_cols(layer * 4 + row, core)], rs_rx.at[layer, y],
                      ps_s.at[layer, row], ps_r.at[layer, y], zl * 8 + row * 2 + core, h)

    def other_columns(j, carry):
        layer, row = order(j)
        i = layer * 4 + row
        at = w_cols(i, 1 - core)
        w[:, at] = mm(n_t[...], gy[:, at]).astype(BF16)
        to_partner(i).start()
        return carry

    lax.fori_loop(0, N_CHIP, other_columns, 0)

    own_w.wait()
    for d in range(1, N_HEAD):
        src = lax.rem(h + d, N_HEAD)
        remote(w_piece(h), wcol.at[src, own_part], wa_s.at[d], wa_r.at[src], c, src).wait_recv()

    def w_half(part, half):
        return wcol.at[:, part, pl.ds(half * (W_ROWS // 2), W_ROWS // 2)]

    def w_y(part, half, to):
        return remote(w_half(part, half), w_half(part, half), wg_s.at[half], wg_r.at[half], to, h)

    def w_core(part, i):
        return remote(wcol.at[:, part], wcol.at[:, part], wg_s.at[2 + i], wg_r.at[2 + i], partner, h)

    w_y(own_part, 0, y_down).start()
    w_y(own_part, 1, y_up).start()
    w_core(own_part, 0).start()

    def own_columns(j, carry):
        layer, row = order(j)
        i = layer * 4 + row
        at = w_cols(i, core)
        product = mm(n_t[...], gy[:, at])
        from_partner(i).wait_recv()
        both = (product + crx[i].astype(F32)).astype(BF16)

        @pl.when(lax.rem(j, 4) < 3)
        def _():
            w[:, at] = both
            to_owner(layer, row).start()

        @pl.when(lax.rem(j, 4) == 3)
        def _():
            rs_rx[layer, y] = both
        return carry

    lax.fori_loop(0, N_CHIP, own_columns, 0)

    run[...] = jnp.zeros_like(run)

    def local_grads(i, carry):
        b = NBLK - 1 - i
        rows = rows_of(b)
        kept = pick(b, jnp.ones_like(keep1), keep1, keep2)
        for hh in range(HEADS):
            cols = cols_of(hh)
            a, g, inv = att[rows, cols], gn[rows, cols], inv_s[rows, hh:hh + 1]
            mean = jnp.mean(g * a, axis=-1, keepdims=True)
            grad = (inv * (g - a * (inv * inv) * mean)).astype(BF16)
            ga[rows, cols] = grad
            col = dsc[rows, hh:hh + 1]
            qw = (q[rows, cols].astype(F32) * jnp.exp(col)).astype(BF16)
            direct = mm(qw, grad, TN)
            gloc[b, hh] = run[hh]
            run[hh] = kept * (direct + jnp.exp(col[BL - 1:BL, :]) * run[hh])
        return carry

    lax.fori_loop(0, NBLK, local_grads, 0)
    for hh in range(HEADS):
        sbuf[1, cols_of(hh), :] = run[hh].astype(BF16)

    pair(1).start()

    arrive(west, 0)
    go(west, 0, 6, east)
    arrive(east, 1)
    go(east, 1, 7, west)

    chip_state(1)
    chip_entry(1)
    own_entry(1)

    def backward(b, carry):
        rows = rows_of(b)
        for hh in range(HEADS):
            cols = cols_of(hh)
            coef1 = keep2 * end_of(2, hh)
            coef = pick(b, keep1 * end_of(1, hh) * coef1, coef1, jnp.ones_like(keep1))
            sg = (gloc[b, hh] + coef * entry[hh]).astype(BF16)
            qb, kb, vb, gb = q[rows, cols], k[rows, cols], v[rows, cols], ga[rows, cols]
            col = dsc[rows, hh:hh + 1]
            tail = jnp.exp(col[BL - 1:BL, :] - col)
            ds = (mm(gb, vb, NT) * mask_of(rows, hh)).astype(BF16)
            gq[rows, cols] = (mm(ds, kb) + jnp.exp(col) * mm(gb, sth[b, hh], NT)).astype(BF16)
            gk[rows, cols] = (mm(ds, qb, TN) + tail * mm(vb, sg, NT)).astype(BF16)
            kw = (kb.astype(F32) * tail).astype(BF16)
            gv[rows, cols] = (mm(pr[b, hh], gb, TN) + mm(kw, sg)).astype(BF16)
        return carry

    lax.fori_loop(0, NBLK, backward, 0)

    for half in range(2):
        arrive(zp, half)
        go(zp, half, 8 + half, east)
        go(zp, half, 10 + half, west)

    w_y(far_part, 0, y_up).wait_recv()
    w_y(far_part, 1, y_down).wait_recv()
    w_core(far_part, 1).start()
    outs = [pltpu.make_async_copy(src, dst, osem.at[i]) for i, (src, dst) in enumerate(
        [(gq, gq_hbm), (gk, gk_hbm), (gv, gv_hbm), (gw, gw_hbm), (out_y, out_y_hbm)])]
    for copy in outs[:3]:
        copy.start()
    w_core(1 - core + 2 * lax.rem(y, 2), 0).wait_recv()
    w_core(1 - core + 2 * (1 - lax.rem(y, 2)), 1).wait_recv()

    def product(slot, start):
        def rows_step(b, carry):
            rows = rows_of(b)
            term = mm(nall[slot, rows, :], wcol[slot].reshape(FEAT, COLS_Y))
            if start:
                acc[rows, :] = term
            else:
                acc[rows, :] += term
            return carry

        lax.fori_loop(0, NBLK, rows_step, 0)

    product(h, True)
    arrive(west, 1)
    product(west, False)
    arrive(east, 0)
    product(east, False)
    for half in range(2):
        arrive(far, half)
        go(far, half, 12 + half, zp)
    product(zp, False)
    product(far, False)

    def from_row(layer, d):
        row = lax.rem(y + d, 4)
        remote(w.at[:, w_cols(layer * 4 + y, core)], rs_rx.at[layer, row], ps_s.at[layer, row],
               ps_r.at[layer, row], c, h).wait_recv()

    def along_y(layer):
        for d in range(1, 4):
            from_row(layer, d)
        return sum(rs_rx[layer, row].astype(F32) for row in range(4))

    def to_layer():
        return remote(rs_rx.at[1 - zl, y], z_rx, z_s, z_r, z_peer, h)

    rs_rx[1 - zl, y] = along_y(1 - zl).astype(BF16)
    to_layer().start()

    arrive(west_z, 0)
    arrive(west_z, 1)
    product(west_z, False)
    arrive(east_z, 0)
    arrive(east_z, 1)
    product(east_z, False)
    gw_mine = along_y(zl)
    to_layer().wait_recv()
    gw[...] = (gw_mine + z_rx[...].astype(F32)).astype(BF16)
    outs[3].start()
    arrive(far_z, 0)
    arrive(far_z, 1)
    product(far_z, False)
    out_y[...] = acc[...].astype(BF16)
    outs[4].start()

    for d in range(1, N_HEAD):
        w_spread(d).wait_send()
    for d in range(1, N_CTX):
        scal_spread(d).wait_send()
    for way in range(2):
        pair(way).wait_send()
        swap(way).wait_send()
        for d in range(1, N_CHIP):
            @pl.when(inside(way, d))
            def _():
                pass_on(way, d).wait_send()
    w_y(own_part, 0, y_down).wait_send()
    w_y(own_part, 1, y_up).wait_send()
    w_core(own_part, 0).wait_send()
    w_core(far_part, 1).wait_send()
    for i in range(N_CHIP):
        to_partner(i).wait_send()
    for layer in range(2):
        for d in range(1, 4):
            to_owner(layer, lax.rem(y + d, 4)).wait_send()
    to_layer().wait_send()
    for copy in sent:
        copy.wait_send()
    for copy in outs:
        copy.wait()


def hand_over(*refs):
    sems = refs[-1]
    count = (len(refs) - 1) // 2
    copies = [pltpu.make_async_copy(refs[i], refs[count + i], sems.at[i]) for i in range(count)]
    for copy in copies:
        copy.start()
    for copy in copies:
        copy.wait()


def per_device(q_in, k_in, v_in, log_decay, block_doc, w_out, grad_y):
    vmem = pl.BlockSpec(memory_space=pltpu.VMEM)
    hbm = pl.BlockSpec(memory_space=pl.ANY)
    dma = pltpu.SemaphoreType.DMA
    head_shape = jax.ShapeDtypeStruct((TOK, FEAT), BF16)
    shapes = (
        jax.ShapeDtypeStruct((TOK, COLS_Y), BF16),
        head_shape, head_shape, head_shape,
        jax.ShapeDtypeStruct((FEAT, COLS_W), BF16),
    )
    heads_vmem = pltpu.VMEM((TOK, FEAT), BF16)
    results = pl.pallas_call(
        kernel,
        out_shape=shapes,
        in_specs=[pl.BlockSpec(memory_space=pltpu.SMEM), vmem] + [hbm] * 5,
        out_specs=(hbm,) * 5,
        scratch_shapes=[
            heads_vmem, heads_vmem, heads_vmem,
            pltpu.VMEM((FEAT, D), BF16),
            pltpu.VMEM((TOK, D), BF16),
            heads_vmem, heads_vmem, heads_vmem,
            pltpu.VMEM((FEAT, COLS_W), BF16),
            pltpu.VMEM((TOK, COLS_Y), BF16),
            pltpu.VMEM((8, DH), F32),
            pltpu.VMEM((TOK, HEADS), F32),
            pltpu.VMEM((HEADS, TOK), F32),
            pltpu.VMEM((HEADS, DH, DH), F32),
            pltpu.VMEM((NBLK, HEADS, DH, DH), F32),
            pltpu.VMEM((NBLK, HEADS, DH, DH), BF16),
            pltpu.VMEM((NBLK, HEADS, DH, DH), F32),
            pltpu.VMEM((NBLK, HEADS, BL, BL), BF16),
            pltpu.VMEM((TOK, FEAT), F32),
            pltpu.VMEM((TOK, FEAT), F32),
            pltpu.VMEM((TOK, HEADS), F32),
            heads_vmem,
            pltpu.VMEM((FEAT, TOK), BF16),
            pltpu.VMEM((N_HEAD, TOK, FEAT), BF16),
            pltpu.VMEM((N_HEAD, W_PARTS, W_ROWS, COLS_Y), BF16),
            pltpu.VMEM((N_CHIP, FEAT, COLS_W), BF16),
            pltpu.VMEM((2, 4, FEAT, COLS_W), BF16),
            pltpu.VMEM((FEAT, COLS_W), BF16),
            pltpu.VMEM((2, FEAT, DH), BF16),
            pltpu.VMEM((2, FEAT, DH), BF16),
            pltpu.VMEM((2, FEAT // 2, DH), BF16),
            pltpu.VMEM((2, N_CHIP, FEAT // 2, DH), BF16),
            pltpu.VMEM((2, FEAT // 2, DH), BF16),
            pltpu.VMEM((2, FEAT // 2, DH), BF16),
            pltpu.VMEM((N_CTX, 8, DH), F32),
            pltpu.VMEM((2, 12, 8, DH), F32),
            pltpu.VMEM((HEADS, DH, DH), F32),
            pltpu.VMEM((TOK, COLS_Y), F32),
            dma((6,)), dma((5,)),
            dma((N_HEAD,)), dma((N_HEAD,)),
            dma((4,)), dma((4,)),
            dma((N_CTX,)), dma((N_CTX,)),
            dma((2, 2)), dma((2, 2)),
            dma((2, N_CHIP)), dma((2, N_CHIP)),
            dma((14,)), dma((N_HEAD, 2)),
            dma((N_CHIP,)), dma((N_CHIP,)),
            dma((2, 4)), dma((2, 4)),
            dma, dma,
        ],
        compiler_params=pltpu.CompilerParams(
            collective_id=0, has_side_effects=True, vmem_limit_bytes=63 << 20),
        name="attention_and_projection",
    )(block_doc, log_decay.T, q_in, k_in, v_in, w_out, grad_y)
    return pl.pallas_call(
        hand_over,
        out_shape=shapes,
        in_specs=[hbm] * 5,
        out_specs=(hbm,) * 5,
        scratch_shapes=[dma((5,))],
        name="results",
    )(*results)


def solution(mesh):
    in_specs = (
        P("ctx", "head"),
        P("ctx", "head"),
        P("ctx", "head"),
        P("ctx", "head"),
        P("ctx"),
        P("head", None),
        P("ctx", None),
    )
    out_specs = (
        P("ctx", "head"),
        P("ctx", "head"),
        P("ctx", "head"),
        P("ctx", "head"),
        P("head", "ctx"),
    )
    return jax.shard_map(
        per_device, mesh=mesh, in_specs=in_specs, out_specs=out_specs, check_vma=False
    )
```

```python
import jax
import jax.numpy as jnp
from jax import lax
from jax.experimental import pallas as pl
from jax.experimental.pallas import tpu as pltpu
from jax.sharding import PartitionSpec as P

DH = 128
BL = 256
EPS = 1e-06
F32 = jnp.float32
BF16 = jnp.bfloat16
MESH = pl.DeviceIdType.MESH

N_CTX = 16
N_HEAD = 8
N_CHIP = 8
NBLK = 3
HEADS = 4
TOK = NBLK * BL
HALF = TOK // 2
FEAT = HEADS * DH
D = 6144
COLS_Y = D // N_HEAD
COLS_W = D // N_CTX
W_PARTS = 4
W_ROWS = FEAT // W_PARTS

NN = (((1,), (0,)), ((), ()))
NT = (((1,), (1,)), ((), ()))
TN = (((0,), (0,)), ((), ()))


def mm(a, b, dims=NN):
    return lax.dot_general(a, b, dims, preferred_element_type=F32)


def kernel(
    docs, ldt, q_hbm, k_hbm, v_hbm, w_hbm, gy_hbm,
    out_y_hbm, gq_hbm, gk_hbm, gv_hbm, gw_hbm,
    q, k, v, w, gy, gq, gk, gv, gw, out_y,
    scal, dsc, dsr, run, loc, sth, gloc, pr, att, gn, inv_s, ga, n_t,
    nall, wcol, crx, rs_rx, z_rx, sbuf, p_rx, cbuf, c_rx, ebuf, e_rx, scal_rx, wgt, entry, acc,
    lsem, osem, wa_s, wa_r, wg_s, wg_r, sc_s, sc_r, x_s, x_r, st_s, st_r,
    ag_s, ag_r, cs_s, cs_r, ps_s, ps_r, z_s, z_r,
):
    c = lax.axis_index("ctx")
    h = lax.axis_index("head")
    chip, core = c // 2, lax.rem(c, 2)
    partner = c + 1 - 2 * core
    zl, y = c // 8, lax.rem(chip, 4)
    y_up = zl * 8 + lax.rem(y + 1, 4) * 2 + core
    y_down = zl * 8 + lax.rem(y + 3, 4) * 2 + core
    z_peer = lax.rem(c + 8, N_CTX)
    own_part = lax.rem(y, 2) * 2 + core
    far_part = (1 - lax.rem(y, 2)) * 2 + core
    hx, hz = h // 2, lax.rem(h, 2)
    east = lax.rem(hx + 1, 4) * 2 + hz
    west = lax.rem(hx + 3, 4) * 2 + hz
    zp = hx * 2 + 1 - hz
    east_z = lax.rem(hx + 1, 4) * 2 + 1 - hz
    west_z = lax.rem(hx + 3, 4) * 2 + 1 - hz
    far = lax.rem(hx + 2, 4) * 2 + hz
    far_z = lax.rem(hx + 2, 4) * 2 + 1 - hz

    def remote(src, dst, ssem, rsem, to_c, to_h):
        return pltpu.make_async_remote_copy(
            src_ref=src, dst_ref=dst, send_sem=ssem, recv_sem=rsem,
            device_id=(to_c, to_h), device_id_type=MESH,
        )

    loads = [
        pltpu.make_async_copy(src, dst, lsem.at[i])
        for i, (src, dst) in enumerate(
            [(k_hbm, k), (v_hbm, v), (q_hbm, q), (w_hbm, w), (gy_hbm, gy)])
    ]

    def w_piece(to):
        return w_hbm.at[pl.ds(pl.multiple_of(own_part * W_ROWS, W_ROWS), W_ROWS),
                        pl.ds(pl.multiple_of(to * COLS_Y, COLS_Y), COLS_Y)]

    own_w = pltpu.make_async_copy(w_piece(h), wcol.at[h, own_part], lsem.at[5])
    for copy in loads[:3]:
        copy.start()

    barrier = pltpu.get_barrier_semaphore()
    for d in range(1, N_CTX):
        pl.semaphore_signal(barrier, inc=1, device_id=(lax.rem(c + d, N_CTX), h),
                            device_id_type=MESH)
    for d in range(1, N_HEAD):
        pl.semaphore_signal(barrier, inc=1, device_id=(c, lax.rem(h + d, N_HEAD)),
                            device_id_type=MESH)
    pl.semaphore_wait(barrier, N_CTX + N_HEAD - 2)

    def w_spread(d):
        to = lax.rem(h + d, N_HEAD)
        return remote(w_piece(to), wcol.at[h, own_part], wa_s.at[d], wa_r.at[h], c, to)

    def scal_spread(d):
        return remote(scal, scal_rx.at[c], sc_s.at[d], sc_r.at[c], lax.rem(c + d, N_CTX), h)

    for copy in loads[3:]:
        copy.start()
    own_w.start()
    at_row = lax.broadcasted_iota(jnp.int32, (BL, BL), 0)
    at_col = lax.broadcasted_iota(jnp.int32, (BL, BL), 1)
    lower = at_row >= at_col

    def doc_row(b):
        return jnp.full((1, DH), docs[b], jnp.int32).astype(F32)

    keep1 = jnp.where(doc_row(0) == doc_row(1), 1.0, 0.0)
    keep2 = jnp.where(doc_row(1) == doc_row(2), 1.0, 0.0)

    def rows_of(b):
        return pl.ds(pl.multiple_of(b * BL, BL), BL)

    def cols_of(hh):
        return slice(hh * DH, (hh + 1) * DH)

    def mask_of(rows, hh):
        gap = dsc[rows, hh:hh + 1] - dsr[hh:hh + 1, rows]
        return jnp.where(lower, jnp.exp(jnp.minimum(gap, 0.0)), 0.0)

    def pick(b, zero, one, two):
        return jnp.where(b == 0, zero, jnp.where(b == 1, one, two))

    run[...] = jnp.zeros_like(run)

    tri = jnp.where(lower, 1.0, 0.0).astype(F32)
    exact = dict(precision=lax.Precision.HIGHEST, preferred_element_type=F32)

    def sums(b, carry):
        rows = rows_of(b)
        dsc[rows, :] = lax.dot_general(tri, ldt[:, rows], NT, **exact)
        dsr[:, rows] = lax.dot_general(ldt[:, rows], tri, NT, **exact)
        return carry

    lax.fori_loop(0, NBLK, sums, 0)
    ends = [dsr[:, (b + 1) * BL - 1:(b + 1) * BL] for b in range(NBLK)]
    scal[0:HEADS, :] = jnp.broadcast_to(ends[0] + ends[1] + ends[2], (HEADS, DH))
    for row, b in ((4, 0), (5, NBLK - 1), (6, 1), (7, 1)):
        scal[row:row + 1, :] = doc_row(b)
    for d in range(1, N_CTX):
        scal_spread(d).start()
    scal_rx[c] = scal[...]

    def local_states(b, carry):
        rows = rows_of(b)
        kept = pick(b, keep1, keep2, jnp.ones_like(keep1))
        for hh in range(HEADS):
            col = dsc[rows, hh:hh + 1]
            end = col[BL - 1:BL, :]
            kw = (k[rows, cols_of(hh)].astype(F32) * jnp.exp(end - col)).astype(BF16)
            update = mm(kw, v[rows, cols_of(hh)], TN)
            loc[b, hh] = run[hh]
            run[hh] = kept * (jnp.exp(end) * run[hh] + update)
        return carry

    loads[0].wait()
    loads[1].wait()
    lax.fori_loop(0, NBLK, local_states, 0)
    for hh in range(HEADS):
        sbuf[0, cols_of(hh), :] = run[hh].astype(BF16)

    def pair(way):
        return remote(sbuf.at[way], p_rx.at[way], x_s.at[way, 0], x_r.at[way, 0], partner, h)

    def pass_on(way, d):
        to = chip - d if way else chip + d
        return remote(cbuf.at[way], c_rx.at[way, chip], st_s.at[way, d], st_r.at[way, chip],
                      2 * to + core, h)

    def swap(way):
        return remote(ebuf.at[way], e_rx.at[way], x_s.at[way, 1], x_r.at[way, 1], partner, h)

    def inside(way, d):
        return (chip >= d) if way else (chip + d < N_CHIP)

    pair(0).start()

    def intra(b, carry):
        rows = rows_of(b)
        for hh in range(HEADS):
            cols = cols_of(hh)
            probs = (mm(q[rows, cols], k[rows, cols], NT) * mask_of(rows, hh)).astype(BF16)
            pr[b, hh] = probs
            att[rows, cols] = mm(probs, v[rows, cols])
        return carry

    loads[2].wait()
    lax.fori_loop(0, NBLK, intra, 0)

    for d in range(1, N_CTX):
        src = lax.rem(c + d, N_CTX)
        remote(scal, scal_rx.at[src], sc_s.at[d], sc_r.at[src], src, h).wait_recv()

    for way in range(2):
        total = jnp.zeros((8, DH), F32)
        mine = scal_rx[2 * chip + 1, 5:6, :] if way else scal_rx[2 * chip, 4:5, :]
        for r in range(N_CHIP) if way else range(N_CHIP - 1, -1, -1):
            theirs = scal_rx[2 * r, 4:5, :] if way else scal_rx[2 * r + 1, 5:6, :]
            here = jnp.where((r > chip) if way else (r < chip), 1.0, 0.0)
            wgt[way, r] = jnp.exp(total) * jnp.where(theirs == mine, here, 0.0)
            total = total + here * (scal_rx[2 * r] + scal_rx[2 * r + 1])

    one = jnp.ones((8, DH), F32)

    def same(row, other):
        return jnp.where(scal_rx[2 * chip, row:row + 1, :] == scal_rx[2 * chip + 1, other:other + 1, :],
                         1.0, 0.0)

    log0, log1 = scal_rx[2 * chip], scal_rx[2 * chip + 1]
    from_core0 = jnp.exp(log1) * same(5, 5)
    from_core1 = jnp.exp(log0) * same(4, 4)
    through0 = jnp.exp(log0) * same(4, 4)
    through1 = jnp.exp(log1) * same(5, 5)
    link = same(5, 4) * one
    is0 = core == 0
    wgt[0, 8] = jnp.where(is0, from_core0, one)
    wgt[0, 9] = jnp.where(is0, one, from_core0)
    wgt[0, 10] = jnp.where(is0, one, through0)
    wgt[0, 11] = jnp.where(is0, 0.0, link)
    wgt[1, 8] = jnp.where(is0, one, from_core1)
    wgt[1, 9] = jnp.where(is0, from_core1, one)
    wgt[1, 10] = jnp.where(is0, through1, one)
    wgt[1, 11] = jnp.where(is0, link, 0.0)

    def head_rows(j):
        return pl.ds(pl.multiple_of((2 * core + j) * DH, DH), DH)

    def chip_state(way):
        pair(way).wait_recv()
        for j in range(2):
            hh = 2 * core + j
            cbuf[way, cols_of(j), :] = (
                wgt[way, 8, pl.ds(hh, 1), :] * run[hh]
                + wgt[way, 9, pl.ds(hh, 1), :] * p_rx[way, head_rows(j), :].astype(F32)
            ).astype(BF16)
        for d in range(1, N_CHIP):
            @pl.when(inside(way, d))
            def _():
                pass_on(way, d).start()

    def chip_entry(way):
        ebuf_f = entry
        for j in range(2):
            ebuf_f[j] = jnp.zeros((DH, DH), F32)

        def add(r, carry):
            @pl.when((r > chip) if way else (r < chip))
            def _():
                remote(cbuf.at[way], c_rx.at[way, r], st_s.at[way, 0], st_r.at[way, r],
                       2 * r + core, h).wait_recv()
                for j in range(2):
                    ebuf_f[j] += (wgt[way, r, pl.ds(2 * core + j, 1), :]
                                  * c_rx[way, r, cols_of(j), :].astype(F32))
            return carry

        lax.fori_loop(0, N_CHIP, add, 0)
        for j in range(2):
            ebuf[way, cols_of(j), :] = ebuf_f[j].astype(BF16)
        swap(way).start()

    def own_entry(way):
        swap(way).wait_recv()
        for j in range(2):
            for hh, chips in ((2 * core + j, ebuf), (2 * (1 - core) + j, e_rx)):
                rows = pl.ds(pl.multiple_of(hh * DH, DH), DH)
                entry[hh] = (wgt[way, 10, pl.ds(hh, 1), :] * chips[way, cols_of(j), :].astype(F32)
                             + wgt[way, 11, pl.ds(hh, 1), :] * p_rx[way, rows, :].astype(F32))

    chip_state(0)

    for d in range(1, N_HEAD):
        w_spread(d).start()

    loads[3].wait()
    loads[4].wait()
    gn[...] = jnp.zeros_like(gn)
    step_k = 1024

    def grad_normed(i, carry):
        at = pl.ds(pl.multiple_of(i * step_k, step_k), step_k)
        gn[...] += mm(gy[:, at], w[:, at], NT)
        return carry

    lax.fori_loop(0, 4, grad_normed, 0)
    chip_entry(0)
    lax.fori_loop(4, D // step_k, grad_normed, 0)
    own_entry(0)

    def end_of(b, hh):
        return jnp.exp(dsc[b * BL + BL - 1:(b + 1) * BL, hh:hh + 1])

    def inter(b, carry):
        rows = rows_of(b)
        for hh in range(HEADS):
            cols = cols_of(hh)
            coef1 = keep1 * end_of(0, hh)
            coef = pick(b, jnp.ones_like(keep1), coef1, keep2 * end_of(1, hh) * coef1)
            state = (loc[b, hh] + coef * entry[hh]).astype(BF16)
            sth[b, hh] = state
            a = att[rows, cols] + jnp.exp(dsc[rows, hh:hh + 1]) * mm(q[rows, cols], state)
            inv = lax.rsqrt(jnp.mean(a * a, axis=-1, keepdims=True) + EPS)
            n = a * inv
            att[rows, cols] = a
            inv_s[rows, hh:hh + 1] = inv
            nall[h, rows, cols] = n.astype(BF16)
            n_t[cols, rows] = n.T.astype(BF16)
        return carry

    lax.fori_loop(0, NBLK, inter, 0)

    def part(slot, half):
        return nall.at[slot, pl.ds(half * HALF, HALF), :]

    def hand(slot, half, sem, to):
        return remote(part(slot, half), part(slot, half), ag_s.at[sem], ag_r.at[slot, half], c, to)

    def arrive(slot, half):
        remote(part(slot, half), part(slot, half), ag_s.at[0], ag_r.at[slot, half], c, zp).wait_recv()

    sent = []

    def go(*args):
        copy = hand(*args)
        copy.start()
        sent.append(copy)

    for half in range(2):
        go(h, half, half, zp)
        go(h, half, 2 + half, east)
        go(h, half, 4 + half, west)

    run[...] = jnp.zeros_like(run)

    def local_grads(i, carry):
        b = NBLK - 1 - i
        rows = rows_of(b)
        kept = pick(b, jnp.ones_like(keep1), keep1, keep2)
        for hh in range(HEADS):
            cols = cols_of(hh)
            a, g, inv = att[rows, cols], gn[rows, cols], inv_s[rows, hh:hh + 1]
            mean = jnp.mean(g * a, axis=-1, keepdims=True)
            grad = (inv * (g - a * (inv * inv) * mean)).astype(BF16)
            ga[rows, cols] = grad
            col = dsc[rows, hh:hh + 1]
            qw = (q[rows, cols].astype(F32) * jnp.exp(col)).astype(BF16)
            direct = mm(qw, grad, TN)
            gloc[b, hh] = run[hh]
            run[hh] = kept * (direct + jnp.exp(col[BL - 1:BL, :]) * run[hh])
        return carry

    lax.fori_loop(0, NBLK, local_grads, 0)
    for hh in range(HEADS):
        sbuf[1, cols_of(hh), :] = run[hh].astype(BF16)

    pair(1).start()

    def w_cols(i, parity):
        return pl.ds(pl.multiple_of((2 * i + parity) * COLS_W, COLS_W), COLS_W)

    def to_partner(i):
        return remote(w.at[:, w_cols(i, 1 - core)], crx.at[i], cs_s.at[i], cs_r.at[i], partner, h)

    def from_partner(i):
        return remote(w.at[:, w_cols(i, core)], crx.at[i], cs_s.at[i], cs_r.at[i], partner, h)

    def order(j):
        return jnp.where(j < 4, 1 - zl, zl), lax.rem(y + 1 + lax.rem(j, 4), 4)

    def to_owner(layer, row):
        return remote(w.at[:, w_cols(layer * 4 + row, core)], rs_rx.at[layer, y],
                      ps_s.at[layer, row], ps_r.at[layer, y], zl * 8 + row * 2 + core, h)

    def other_columns(j, carry):
        layer, row = order(j)
        i = layer * 4 + row
        at = w_cols(i, 1 - core)
        w[:, at] = mm(n_t[...], gy[:, at]).astype(BF16)
        to_partner(i).start()
        return carry

    lax.fori_loop(0, N_CHIP, other_columns, 0)

    chip_state(1)

    own_w.wait()
    for d in range(1, N_HEAD):
        src = lax.rem(h + d, N_HEAD)
        remote(w_piece(h), wcol.at[src, own_part], wa_s.at[d], wa_r.at[src], c, src).wait_recv()

    def w_half(part, half):
        return wcol.at[:, part, pl.ds(half * (W_ROWS // 2), W_ROWS // 2)]

    def w_y(part, half, to):
        return remote(w_half(part, half), w_half(part, half), wg_s.at[half], wg_r.at[half], to, h)

    def w_core(part, i):
        return remote(wcol.at[:, part], wcol.at[:, part], wg_s.at[2 + i], wg_r.at[2 + i], partner, h)

    w_y(own_part, 0, y_down).start()
    w_y(own_part, 1, y_up).start()
    w_core(own_part, 0).start()

    def own_columns(j, carry):
        layer, row = order(j)
        i = layer * 4 + row
        at = w_cols(i, core)
        product = mm(n_t[...], gy[:, at])
        from_partner(i).wait_recv()
        both = (product + crx[i].astype(F32)).astype(BF16)

        @pl.when(lax.rem(j, 4) < 3)
        def _():
            w[:, at] = both
            to_owner(layer, row).start()

        @pl.when(lax.rem(j, 4) == 3)
        def _():
            rs_rx[layer, y] = both
        return carry

    lax.fori_loop(0, N_CHIP, own_columns, 0)

    arrive(west, 0)
    go(west, 0, 6, east)
    arrive(east, 1)
    go(east, 1, 7, west)
    chip_entry(1)
    arrive(zp, 0)
    go(zp, 0, 8, east)
    go(zp, 0, 10, west)
    own_entry(1)

    def backward(b, carry):
        rows = rows_of(b)
        for hh in range(HEADS):
            cols = cols_of(hh)
            coef1 = keep2 * end_of(2, hh)
            coef = pick(b, keep1 * end_of(1, hh) * coef1, coef1, jnp.ones_like(keep1))
            sg = (gloc[b, hh] + coef * entry[hh]).astype(BF16)
            qb, kb, vb, gb = q[rows, cols], k[rows, cols], v[rows, cols], ga[rows, cols]
            col = dsc[rows, hh:hh + 1]
            tail = jnp.exp(col[BL - 1:BL, :] - col)
            ds = (mm(gb, vb, NT) * mask_of(rows, hh)).astype(BF16)
            gq[rows, cols] = (mm(ds, kb) + jnp.exp(col) * mm(gb, sth[b, hh], NT)).astype(BF16)
            gk[rows, cols] = (mm(ds, qb, TN) + tail * mm(vb, sg, NT)).astype(BF16)
            kw = (kb.astype(F32) * tail).astype(BF16)
            gv[rows, cols] = (mm(pr[b, hh], gb, TN) + mm(kw, sg)).astype(BF16)
        return carry

    lax.fori_loop(0, NBLK, backward, 0)

    arrive(zp, 1)
    go(zp, 1, 9, east)
    go(zp, 1, 11, west)

    w_y(far_part, 0, y_up).wait_recv()
    w_y(far_part, 1, y_down).wait_recv()
    w_core(far_part, 1).start()
    outs = [pltpu.make_async_copy(src, dst, osem.at[i]) for i, (src, dst) in enumerate(
        [(gq, gq_hbm), (gk, gk_hbm), (gv, gv_hbm), (gw, gw_hbm), (out_y, out_y_hbm)])]
    for copy in outs[:3]:
        copy.start()
    w_core(1 - core + 2 * lax.rem(y, 2), 0).wait_recv()
    w_core(1 - core + 2 * (1 - lax.rem(y, 2)), 1).wait_recv()

    def product(slot, start):
        def rows_step(b, carry):
            rows = rows_of(b)
            term = mm(nall[slot, rows, :], wcol[slot].reshape(FEAT, COLS_Y))
            if start:
                acc[rows, :] = term
            else:
                acc[rows, :] += term
            return carry

        lax.fori_loop(0, NBLK, rows_step, 0)

    product(h, True)
    arrive(west, 1)
    product(west, False)
    arrive(east, 0)
    product(east, False)
    for half in range(2):
        arrive(far, half)
        go(far, half, 12 + half, zp)
    product(zp, False)
    product(far, False)

    def from_row(layer, d):
        row = lax.rem(y + d, 4)
        remote(w.at[:, w_cols(layer * 4 + y, core)], rs_rx.at[layer, row], ps_s.at[layer, row],
               ps_r.at[layer, row], c, h).wait_recv()

    def along_y(layer):
        for d in range(1, 4):
            from_row(layer, d)
        return sum(rs_rx[layer, row].astype(F32) for row in range(4))

    def to_layer():
        return remote(rs_rx.at[1 - zl, y], z_rx, z_s, z_r, z_peer, h)

    rs_rx[1 - zl, y] = along_y(1 - zl).astype(BF16)
    to_layer().start()

    arrive(west_z, 0)
    arrive(west_z, 1)
    product(west_z, False)
    arrive(east_z, 0)
    arrive(east_z, 1)
    product(east_z, False)
    gw_mine = along_y(zl)
    to_layer().wait_recv()
    gw[...] = (gw_mine + z_rx[...].astype(F32)).astype(BF16)
    outs[3].start()
    arrive(far_z, 0)
    arrive(far_z, 1)
    product(far_z, False)
    out_y[...] = acc[...].astype(BF16)
    outs[4].start()

    for d in range(1, N_HEAD):
        w_spread(d).wait_send()
    for d in range(1, N_CTX):
        scal_spread(d).wait_send()
    for way in range(2):
        pair(way).wait_send()
        swap(way).wait_send()
        for d in range(1, N_CHIP):
            @pl.when(inside(way, d))
            def _():
                pass_on(way, d).wait_send()
    w_y(own_part, 0, y_down).wait_send()
    w_y(own_part, 1, y_up).wait_send()
    w_core(own_part, 0).wait_send()
    w_core(far_part, 1).wait_send()
    for i in range(N_CHIP):
        to_partner(i).wait_send()
    for layer in range(2):
        for d in range(1, 4):
            to_owner(layer, lax.rem(y + d, 4)).wait_send()
    to_layer().wait_send()
    for copy in sent:
        copy.wait_send()
    for copy in outs:
        copy.wait()


def hand_over(*refs):
    count = len(refs) // 2
    for src, dst in zip(refs[:count], refs[count:]):
        dst[...] = src[...]


def per_device(q_in, k_in, v_in, log_decay, block_doc, w_out, grad_y):
    vmem = pl.BlockSpec(memory_space=pltpu.VMEM)
    hbm = pl.BlockSpec(memory_space=pl.ANY)
    dma = pltpu.SemaphoreType.DMA
    head_shape = jax.ShapeDtypeStruct((TOK, FEAT), BF16)
    shapes = (
        jax.ShapeDtypeStruct((TOK, COLS_Y), BF16),
        head_shape, head_shape, head_shape,
        jax.ShapeDtypeStruct((FEAT, COLS_W), BF16),
    )
    heads_vmem = pltpu.VMEM((TOK, FEAT), BF16)
    results = pl.pallas_call(
        kernel,
        out_shape=shapes,
        in_specs=[pl.BlockSpec(memory_space=pltpu.SMEM), vmem] + [hbm] * 5,
        out_specs=(hbm,) * 5,
        scratch_shapes=[
            heads_vmem, heads_vmem, heads_vmem,
            pltpu.VMEM((FEAT, D), BF16),
            pltpu.VMEM((TOK, D), BF16),
            heads_vmem, heads_vmem, heads_vmem,
            pltpu.VMEM((FEAT, COLS_W), BF16),
            pltpu.VMEM((TOK, COLS_Y), BF16),
            pltpu.VMEM((8, DH), F32),
            pltpu.VMEM((TOK, HEADS), F32),
            pltpu.VMEM((HEADS, TOK), F32),
            pltpu.VMEM((HEADS, DH, DH), F32),
            pltpu.VMEM((NBLK, HEADS, DH, DH), F32),
            pltpu.VMEM((NBLK, HEADS, DH, DH), BF16),
            pltpu.VMEM((NBLK, HEADS, DH, DH), F32),
            pltpu.VMEM((NBLK, HEADS, BL, BL), BF16),
            pltpu.VMEM((TOK, FEAT), F32),
            pltpu.VMEM((TOK, FEAT), F32),
            pltpu.VMEM((TOK, HEADS), F32),
            heads_vmem,
            pltpu.VMEM((FEAT, TOK), BF16),
            pltpu.VMEM((N_HEAD, TOK, FEAT), BF16),
            pltpu.VMEM((N_HEAD, W_PARTS, W_ROWS, COLS_Y), BF16),
            pltpu.VMEM((N_CHIP, FEAT, COLS_W), BF16),
            pltpu.VMEM((2, 4, FEAT, COLS_W), BF16),
            pltpu.VMEM((FEAT, COLS_W), BF16),
            pltpu.VMEM((2, FEAT, DH), BF16),
            pltpu.VMEM((2, FEAT, DH), BF16),
            pltpu.VMEM((2, FEAT // 2, DH), BF16),
            pltpu.VMEM((2, N_CHIP, FEAT // 2, DH), BF16),
            pltpu.VMEM((2, FEAT // 2, DH), BF16),
            pltpu.VMEM((2, FEAT // 2, DH), BF16),
            pltpu.VMEM((N_CTX, 8, DH), F32),
            pltpu.VMEM((2, 12, 8, DH), F32),
            pltpu.VMEM((HEADS, DH, DH), F32),
            pltpu.VMEM((TOK, COLS_Y), F32),
            dma((6,)), dma((5,)),
            dma((N_HEAD,)), dma((N_HEAD,)),
            dma((4,)), dma((4,)),
            dma((N_CTX,)), dma((N_CTX,)),
            dma((2, 2)), dma((2, 2)),
            dma((2, N_CHIP)), dma((2, N_CHIP)),
            dma((14,)), dma((N_HEAD, 2)),
            dma((N_CHIP,)), dma((N_CHIP,)),
            dma((2, 4)), dma((2, 4)),
            dma, dma,
        ],
        compiler_params=pltpu.CompilerParams(
            collective_id=0, has_side_effects=True, vmem_limit_bytes=63 << 20),
        name="attention_and_projection",
    )(block_doc, log_decay.T, q_in, k_in, v_in, w_out, grad_y)
    steps = 4
    specs = tuple(
        pl.BlockSpec((one.shape[0] // steps, one.shape[1]), lambda i: (i, 0)) for one in shapes)
    return pl.pallas_call(
        hand_over,
        out_shape=shapes,
        grid=(steps,),
        in_specs=specs,
        out_specs=specs,
        name="results",
    )(*results)


def solution(mesh):
    in_specs = (
        P("ctx", "head"),
        P("ctx", "head"),
        P("ctx", "head"),
        P("ctx", "head"),
        P("ctx"),
        P("head", None),
        P("ctx", None),
    )
    out_specs = (
        P("ctx", "head"),
        P("ctx", "head"),
        P("ctx", "head"),
        P("ctx", "head"),
        P("head", "ctx"),
    )
    return jax.shard_map(
        per_device, mesh=mesh, in_specs=in_specs, out_specs=out_specs, check_vma=False
    )
```

```python
import jax
import jax.numpy as jnp
from jax import lax
from jax.experimental import pallas as pl
from jax.experimental.pallas import tpu as pltpu
from jax.sharding import PartitionSpec as P

DH = 128
BL = 256
EPS = 1e-06
F32 = jnp.float32
BF16 = jnp.bfloat16
MESH = pl.DeviceIdType.MESH

N_CTX = 16
N_HEAD = 8
N_CHIP = 8
NBLK = 3
HEADS = 4
TOK = NBLK * BL
HALF = TOK // 2
FEAT = HEADS * DH
D = 6144
COLS_Y = D // N_HEAD
COLS_W = D // N_CTX
W_PARTS = 4
W_ROWS = FEAT // W_PARTS

NN = (((1,), (0,)), ((), ()))
NT = (((1,), (1,)), ((), ()))
TN = (((0,), (0,)), ((), ()))


def mm(a, b, dims=NN):
    return lax.dot_general(a, b, dims, preferred_element_type=F32)


def kernel(
    docs, ldt, q_hbm, k_hbm, v_hbm, w_hbm, gy_hbm,
    out_y_hbm, gq_hbm, gk_hbm, gv_hbm, gw_hbm,
    q, k, v, w, gy, gq, gk, gv, gw, out_y,
    scal, dsc, dsr, run, loc, sth, gloc, pr, att, gn, inv_s, ga, n_t,
    nall, wcol, crx, rs_rx, z_rx, sbuf, p_rx, cbuf, c_rx, ebuf, e_rx, scal_rx, wgt, entry, acc,
    lsem, osem, wa_s, wa_r, wg_s, wg_r, sc_s, sc_r, x_s, x_r, st_s, st_r,
    ag_s, ag_r, cs_s, cs_r, ps_s, ps_r, z_s, z_r,
):
    c = lax.axis_index("ctx")
    h = lax.axis_index("head")
    chip, core = c // 2, lax.rem(c, 2)
    partner = c + 1 - 2 * core
    zl, y = c // 8, lax.rem(chip, 4)
    y_up = zl * 8 + lax.rem(y + 1, 4) * 2 + core
    y_down = zl * 8 + lax.rem(y + 3, 4) * 2 + core
    z_peer = lax.rem(c + 8, N_CTX)
    own_part = lax.rem(y, 2) * 2 + core
    far_part = (1 - lax.rem(y, 2)) * 2 + core
    hx, hz = h // 2, lax.rem(h, 2)
    east = lax.rem(hx + 1, 4) * 2 + hz
    west = lax.rem(hx + 3, 4) * 2 + hz
    zp = hx * 2 + 1 - hz
    east_z = lax.rem(hx + 1, 4) * 2 + 1 - hz
    west_z = lax.rem(hx + 3, 4) * 2 + 1 - hz
    far = lax.rem(hx + 2, 4) * 2 + hz
    far_z = lax.rem(hx + 2, 4) * 2 + 1 - hz

    def remote(src, dst, ssem, rsem, to_c, to_h):
        return pltpu.make_async_remote_copy(
            src_ref=src, dst_ref=dst, send_sem=ssem, recv_sem=rsem,
            device_id=(to_c, to_h), device_id_type=MESH,
        )

    loads = [
        pltpu.make_async_copy(src, dst, lsem.at[i])
        for i, (src, dst) in enumerate(
            [(k_hbm, k), (v_hbm, v), (q_hbm, q)])
    ]
    step_k = 1024
    steps_k = D // step_k

    def load_columns(i):
        at = pl.ds(pl.multiple_of(i * step_k, step_k), step_k)
        return [
            pltpu.make_async_copy(w_hbm.at[:, at], w.at[:, at], lsem.at[4 + i]),
            pltpu.make_async_copy(gy_hbm.at[:, at], gy.at[:, at], lsem.at[4 + steps_k + i]),
        ]


    def w_piece(to):
        return w_hbm.at[pl.ds(pl.multiple_of(own_part * W_ROWS, W_ROWS), W_ROWS),
                        pl.ds(pl.multiple_of(to * COLS_Y, COLS_Y), COLS_Y)]

    own_w = pltpu.make_async_copy(w_piece(h), wcol.at[h, own_part], lsem.at[3])
    for copy in loads:
        copy.start()

    def w_peer(d):
        to_x, to_z = lax.rem(hx + d // 2, 4), lax.rem(hz + d % 2, 2)
        return (z_peer if d % 2 else c), to_x * 2 + to_z

    barrier = pltpu.get_barrier_semaphore()
    for d in range(1, N_HEAD, 2):
        pl.semaphore_signal(barrier, inc=1, device_id=w_peer(d), device_id_type=MESH)
    for d in range(1, N_CTX):
        pl.semaphore_signal(barrier, inc=1, device_id=(lax.rem(c + d, N_CTX), h),
                            device_id_type=MESH)
    for d in range(1, N_HEAD):
        pl.semaphore_signal(barrier, inc=1, device_id=(c, lax.rem(h + d, N_HEAD)),
                            device_id_type=MESH)
    pl.semaphore_wait(barrier, N_CTX + N_HEAD - 2 + N_HEAD // 2)

    def w_spread(d):
        to_c, to = w_peer(d)
        return remote(w_piece(to), wcol.at[h, own_part], wa_s.at[d], wa_r.at[h], to_c, to)

    def scal_spread(d):
        return remote(scal, scal_rx.at[c], sc_s.at[d], sc_r.at[c], lax.rem(c + d, N_CTX), h)

    own_w.start()
    for d in range(1, N_HEAD):
        w_spread(d).start()
    for i in range(steps_k):
        for copy in load_columns(i):
            copy.start()
    at_row = lax.broadcasted_iota(jnp.int32, (BL, BL), 0)
    at_col = lax.broadcasted_iota(jnp.int32, (BL, BL), 1)
    lower = at_row >= at_col

    def doc_row(b):
        return jnp.full((1, DH), docs[b], jnp.int32).astype(F32)

    keep1 = jnp.where(doc_row(0) == doc_row(1), 1.0, 0.0)
    keep2 = jnp.where(doc_row(1) == doc_row(2), 1.0, 0.0)

    def rows_of(b):
        return pl.ds(pl.multiple_of(b * BL, BL), BL)

    def cols_of(hh):
        return slice(hh * DH, (hh + 1) * DH)

    def mask_of(rows, hh):
        gap = dsc[rows, hh:hh + 1] - dsr[hh:hh + 1, rows]
        return jnp.where(lower, jnp.exp(jnp.minimum(gap, 0.0)), 0.0)

    def pick(b, zero, one, two):
        return jnp.where(b == 0, zero, jnp.where(b == 1, one, two))

    run[...] = jnp.zeros_like(run)

    tri = jnp.where(lower, 1.0, 0.0).astype(F32)
    exact = dict(precision=lax.Precision.HIGHEST, preferred_element_type=F32)

    def sums(b, carry):
        rows = rows_of(b)
        dsc[rows, :] = lax.dot_general(tri, ldt[:, rows], NT, **exact)
        dsr[:, rows] = lax.dot_general(ldt[:, rows], tri, NT, **exact)
        return carry

    lax.fori_loop(0, NBLK, sums, 0)
    ends = [dsr[:, (b + 1) * BL - 1:(b + 1) * BL] for b in range(NBLK)]
    scal[0:HEADS, :] = jnp.broadcast_to(ends[0] + ends[1] + ends[2], (HEADS, DH))
    for row, b in ((4, 0), (5, NBLK - 1), (6, 1), (7, 1)):
        scal[row:row + 1, :] = doc_row(b)
    for d in range(1, N_CTX):
        scal_spread(d).start()
    scal_rx[c] = scal[...]

    def local_states(b, carry):
        rows = rows_of(b)
        kept = pick(b, keep1, keep2, jnp.ones_like(keep1))
        for hh in range(HEADS):
            col = dsc[rows, hh:hh + 1]
            end = col[BL - 1:BL, :]
            kw = (k[rows, cols_of(hh)].astype(F32) * jnp.exp(end - col)).astype(BF16)
            update = mm(kw, v[rows, cols_of(hh)], TN)
            loc[b, hh] = run[hh]
            run[hh] = kept * (jnp.exp(end) * run[hh] + update)
        return carry

    loads[0].wait()
    loads[1].wait()
    lax.fori_loop(0, NBLK, local_states, 0)
    for hh in range(HEADS):
        sbuf[0, cols_of(hh), :] = run[hh].astype(BF16)

    def pair(way):
        return remote(sbuf.at[way], p_rx.at[way], x_s.at[way, 0], x_r.at[way, 0], partner, h)

    def pass_on(way, d):
        to = chip - d if way else chip + d
        return remote(cbuf.at[way], c_rx.at[way, chip], st_s.at[way, d], st_r.at[way, chip],
                      2 * to + core, h)

    def swap(way):
        return remote(ebuf.at[way], e_rx.at[way], x_s.at[way, 1], x_r.at[way, 1], partner, h)

    def inside(way, d):
        return (chip >= d) if way else (chip + d < N_CHIP)

    pair(0).start()

    def intra(b, carry):
        rows = rows_of(b)
        for hh in range(HEADS):
            cols = cols_of(hh)
            probs = (mm(q[rows, cols], k[rows, cols], NT) * mask_of(rows, hh)).astype(BF16)
            pr[b, hh] = probs
            att[rows, cols] = mm(probs, v[rows, cols])
        return carry

    loads[2].wait()
    lax.fori_loop(0, NBLK, intra, 0)

    for d in range(1, N_CTX):
        src = lax.rem(c + d, N_CTX)
        remote(scal, scal_rx.at[src], sc_s.at[d], sc_r.at[src], src, h).wait_recv()

    for way in range(2):
        total = jnp.zeros((8, DH), F32)
        mine = scal_rx[2 * chip + 1, 5:6, :] if way else scal_rx[2 * chip, 4:5, :]
        for r in range(N_CHIP) if way else range(N_CHIP - 1, -1, -1):
            theirs = scal_rx[2 * r, 4:5, :] if way else scal_rx[2 * r + 1, 5:6, :]
            here = jnp.where((r > chip) if way else (r < chip), 1.0, 0.0)
            wgt[way, r] = jnp.exp(total) * jnp.where(theirs == mine, here, 0.0)
            total = total + here * (scal_rx[2 * r] + scal_rx[2 * r + 1])

    one = jnp.ones((8, DH), F32)

    def same(row, other):
        return jnp.where(scal_rx[2 * chip, row:row + 1, :] == scal_rx[2 * chip + 1, other:other + 1, :],
                         1.0, 0.0)

    log0, log1 = scal_rx[2 * chip], scal_rx[2 * chip + 1]
    from_core0 = jnp.exp(log1) * same(5, 5)
    from_core1 = jnp.exp(log0) * same(4, 4)
    through0 = jnp.exp(log0) * same(4, 4)
    through1 = jnp.exp(log1) * same(5, 5)
    link = same(5, 4) * one
    is0 = core == 0
    wgt[0, 8] = jnp.where(is0, from_core0, one)
    wgt[0, 9] = jnp.where(is0, one, from_core0)
    wgt[0, 10] = jnp.where(is0, one, through0)
    wgt[0, 11] = jnp.where(is0, 0.0, link)
    wgt[1, 8] = jnp.where(is0, one, from_core1)
    wgt[1, 9] = jnp.where(is0, from_core1, one)
    wgt[1, 10] = jnp.where(is0, through1, one)
    wgt[1, 11] = jnp.where(is0, link, 0.0)

    def head_rows(j):
        return pl.ds(pl.multiple_of((2 * core + j) * DH, DH), DH)

    def chip_state(way):
        pair(way).wait_recv()
        for j in range(2):
            hh = 2 * core + j
            cbuf[way, cols_of(j), :] = (
                wgt[way, 8, pl.ds(hh, 1), :] * run[hh]
                + wgt[way, 9, pl.ds(hh, 1), :] * p_rx[way, head_rows(j), :].astype(F32)
            ).astype(BF16)
        for d in range(1, N_CHIP):
            @pl.when(inside(way, d))
            def _():
                pass_on(way, d).start()

    def chip_entry(way):
        ebuf_f = entry
        for j in range(2):
            ebuf_f[j] = jnp.zeros((DH, DH), F32)

        def add(r, carry):
            @pl.when((r > chip) if way else (r < chip))
            def _():
                remote(cbuf.at[way], c_rx.at[way, r], st_s.at[way, 0], st_r.at[way, r],
                       2 * r + core, h).wait_recv()
                for j in range(2):
                    ebuf_f[j] += (wgt[way, r, pl.ds(2 * core + j, 1), :]
                                  * c_rx[way, r, cols_of(j), :].astype(F32))
            return carry

        lax.fori_loop(0, N_CHIP, add, 0)
        for j in range(2):
            ebuf[way, cols_of(j), :] = ebuf_f[j].astype(BF16)
        swap(way).start()

    def own_entry(way):
        swap(way).wait_recv()
        for j in range(2):
            for hh, chips in ((2 * core + j, ebuf), (2 * (1 - core) + j, e_rx)):
                rows = pl.ds(pl.multiple_of(hh * DH, DH), DH)
                entry[hh] = (wgt[way, 10, pl.ds(hh, 1), :] * chips[way, cols_of(j), :].astype(F32)
                             + wgt[way, 11, pl.ds(hh, 1), :] * p_rx[way, rows, :].astype(F32))

    chip_state(0)


    gn[...] = jnp.zeros_like(gn)

    def grad_normed(i, carry):
        for copy in load_columns(i):
            copy.wait()
        at = pl.ds(pl.multiple_of(i * step_k, step_k), step_k)
        gn[...] += mm(gy[:, at], w[:, at], NT)
        return carry

    lax.fori_loop(0, 4, grad_normed, 0)
    chip_entry(0)
    lax.fori_loop(4, D // step_k, grad_normed, 0)
    own_entry(0)

    def end_of(b, hh):
        return jnp.exp(dsc[b * BL + BL - 1:(b + 1) * BL, hh:hh + 1])

    def inter(b, carry):
        rows = rows_of(b)
        for hh in range(HEADS):
            cols = cols_of(hh)
            coef1 = keep1 * end_of(0, hh)
            coef = pick(b, jnp.ones_like(keep1), coef1, keep2 * end_of(1, hh) * coef1)
            state = (loc[b, hh] + coef * entry[hh]).astype(BF16)
            sth[b, hh] = state
            a = att[rows, cols] + jnp.exp(dsc[rows, hh:hh + 1]) * mm(q[rows, cols], state)
            inv = lax.rsqrt(jnp.mean(a * a, axis=-1, keepdims=True) + EPS)
            n = a * inv
            att[rows, cols] = a
            inv_s[rows, hh:hh + 1] = inv
            nall[h, rows, cols] = n.astype(BF16)
            n_t[cols, rows] = n.T.astype(BF16)
        return carry

    lax.fori_loop(0, NBLK, inter, 0)

    def part(slot, half):
        return nall.at[slot, pl.ds(half * HALF, HALF), :]

    def hand(slot, half, sem, to):
        return remote(part(slot, half), part(slot, half), ag_s.at[sem], ag_r.at[slot, half], c, to)

    def arrive(slot, half):
        remote(part(slot, half), part(slot, half), ag_s.at[0], ag_r.at[slot, half], c, zp).wait_recv()

    sent = []

    def go(*args):
        copy = hand(*args)
        copy.start()
        sent.append(copy)

    for half in range(2):
        go(h, half, half, zp)
        go(h, half, 2 + half, east)
        go(h, half, 4 + half, west)

    run[...] = jnp.zeros_like(run)

    def local_grads(i, carry):
        b = NBLK - 1 - i
        rows = rows_of(b)
        kept = pick(b, jnp.ones_like(keep1), keep1, keep2)
        for hh in range(HEADS):
            cols = cols_of(hh)
            a, g, inv = att[rows, cols], gn[rows, cols], inv_s[rows, hh:hh + 1]
            mean = jnp.mean(g * a, axis=-1, keepdims=True)
            grad = (inv * (g - a * (inv * inv) * mean)).astype(BF16)
            ga[rows, cols] = grad
            col = dsc[rows, hh:hh + 1]
            qw = (q[rows, cols].astype(F32) * jnp.exp(col)).astype(BF16)
            direct = mm(qw, grad, TN)
            gloc[b, hh] = run[hh]
            run[hh] = kept * (direct + jnp.exp(col[BL - 1:BL, :]) * run[hh])
        return carry

    lax.fori_loop(0, NBLK, local_grads, 0)
    for hh in range(HEADS):
        sbuf[1, cols_of(hh), :] = run[hh].astype(BF16)

    pair(1).start()

    def w_cols(i, parity):
        return pl.ds(pl.multiple_of((2 * i + parity) * COLS_W, COLS_W), COLS_W)

    def to_partner(i):
        return remote(w.at[:, w_cols(i, 1 - core)], crx.at[i], cs_s.at[i], cs_r.at[i], partner, h)

    def from_partner(i):
        return remote(w.at[:, w_cols(i, core)], crx.at[i], cs_s.at[i], cs_r.at[i], partner, h)

    def order(j):
        return jnp.where(j < 4, 1 - zl, zl), lax.rem(y + 1 + lax.rem(j, 4), 4)

    def to_owner(layer, row):
        return remote(w.at[:, w_cols(layer * 4 + row, core)], rs_rx.at[layer, y],
                      ps_s.at[layer, row], ps_r.at[layer, y], zl * 8 + row * 2 + core, h)

    def columns(j, carry):
        layer, row = order(j)
        i = layer * 4 + row
        at = pl.ds(pl.multiple_of(i * 2 * COLS_W, 2 * COLS_W), 2 * COLS_W)
        w[:, at] = mm(n_t[...], gy[:, at]).astype(BF16)
        to_partner(i).start()
        return carry

    def chip_sum(j):
        layer, row = order(j)
        i = layer * 4 + row
        at = w_cols(i, core)
        from_partner(i).wait_recv()
        both = (w[:, at].astype(F32) + crx[i].astype(F32)).astype(BF16)

        @pl.when(lax.rem(j, 4) < 3)
        def _():
            w[:, at] = both
            to_owner(layer, row).start()

        @pl.when(lax.rem(j, 4) == 3)
        def _():
            rs_rx[layer, y] = both

    def columns_and_sum(j, carry):
        columns(j, carry)
        chip_sum(j - 2)
        return carry

    lax.fori_loop(0, 2, columns, 0)
    chip_state(1)

    own_w.wait()
    for d in range(1, N_HEAD):
        from_c, src = w_peer(d)
        remote(w_piece(h), wcol.at[src, own_part], wa_s.at[d], wa_r.at[src], from_c, src).wait_recv()

    def w_half(part, half):
        return wcol.at[:, part, pl.ds(half * (W_ROWS // 2), W_ROWS // 2)]

    def w_y(part, half, to):
        return remote(w_half(part, half), w_half(part, half), wg_s.at[half], wg_r.at[half], to, h)

    def w_core(part, i):
        return remote(wcol.at[:, part], wcol.at[:, part], wg_s.at[2 + i], wg_r.at[2 + i], partner, h)

    w_y(own_part, 0, y_down).start()
    w_y(own_part, 1, y_up).start()
    w_core(own_part, 0).start()

    lax.fori_loop(2, N_CHIP, columns_and_sum, 0)
    chip_sum(jnp.int32(N_CHIP - 2))
    chip_sum(jnp.int32(N_CHIP - 1))

    arrive(west, 0)
    go(west, 0, 6, east)
    arrive(east, 1)
    go(east, 1, 7, west)
    chip_entry(1)
    arrive(zp, 0)
    go(zp, 0, 8, east)
    go(zp, 0, 10, west)
    own_entry(1)

    def backward(b, carry):
        rows = rows_of(b)
        for hh in range(HEADS):
            cols = cols_of(hh)
            coef1 = keep2 * end_of(2, hh)
            coef = pick(b, keep1 * end_of(1, hh) * coef1, coef1, jnp.ones_like(keep1))
            sg = (gloc[b, hh] + coef * entry[hh]).astype(BF16)
            qb, kb, vb, gb = q[rows, cols], k[rows, cols], v[rows, cols], ga[rows, cols]
            col = dsc[rows, hh:hh + 1]
            tail = jnp.exp(col[BL - 1:BL, :] - col)
            ds = (mm(gb, vb, NT) * mask_of(rows, hh)).astype(BF16)
            gq[rows, cols] = (mm(ds, kb) + jnp.exp(col) * mm(gb, sth[b, hh], NT)).astype(BF16)
            gk[rows, cols] = (mm(ds, qb, TN) + tail * mm(vb, sg, NT)).astype(BF16)
            kw = (kb.astype(F32) * tail).astype(BF16)
            gv[rows, cols] = (mm(pr[b, hh], gb, TN) + mm(kw, sg)).astype(BF16)
        return carry

    lax.fori_loop(0, NBLK, backward, 0)

    arrive(zp, 1)
    go(zp, 1, 9, east)
    go(zp, 1, 11, west)

    w_y(far_part, 0, y_up).wait_recv()
    w_y(far_part, 1, y_down).wait_recv()
    w_core(far_part, 1).start()
    outs = [pltpu.make_async_copy(src, dst, osem.at[i]) for i, (src, dst) in enumerate(
        [(gq, gq_hbm), (gk, gk_hbm), (gv, gv_hbm), (gw, gw_hbm), (out_y, out_y_hbm)])]
    for copy in outs[:3]:
        copy.start()
    w_core(1 - core + 2 * lax.rem(y, 2), 0).wait_recv()
    w_core(1 - core + 2 * (1 - lax.rem(y, 2)), 1).wait_recv()

    def product(slot, start):
        def rows_step(b, carry):
            rows = rows_of(b)
            term = mm(nall[slot, rows, :], wcol[slot].reshape(FEAT, COLS_Y))
            if start:
                acc[rows, :] = term
            else:
                acc[rows, :] += term
            return carry

        lax.fori_loop(0, NBLK, rows_step, 0)

    product(h, True)
    arrive(west, 1)
    product(west, False)
    arrive(east, 0)
    product(east, False)
    for half in range(2):
        arrive(far, half)
        go(far, half, 12 + half, zp)
    product(zp, False)
    product(far, False)

    def from_row(layer, d):
        row = lax.rem(y + d, 4)
        remote(w.at[:, w_cols(layer * 4 + y, core)], rs_rx.at[layer, row], ps_s.at[layer, row],
               ps_r.at[layer, row], c, h).wait_recv()

    def along_y(layer):
        for d in range(1, 4):
            from_row(layer, d)
        return sum(rs_rx[layer, row].astype(F32) for row in range(4))

    def to_layer():
        return remote(rs_rx.at[1 - zl, y], z_rx, z_s, z_r, z_peer, h)

    rs_rx[1 - zl, y] = along_y(1 - zl).astype(BF16)
    to_layer().start()

    arrive(west_z, 0)
    arrive(west_z, 1)
    product(west_z, False)
    arrive(east_z, 0)
    arrive(east_z, 1)
    product(east_z, False)
    gw_mine = along_y(zl)
    to_layer().wait_recv()
    gw[...] = (gw_mine + z_rx[...].astype(F32)).astype(BF16)
    outs[3].start()
    arrive(far_z, 0)
    arrive(far_z, 1)
    product(far_z, False)
    out_y[...] = acc[...].astype(BF16)
    outs[4].start()

    for d in range(1, N_HEAD):
        w_spread(d).wait_send()
    for d in range(1, N_CTX):
        scal_spread(d).wait_send()
    for way in range(2):
        pair(way).wait_send()
        swap(way).wait_send()
        for d in range(1, N_CHIP):
            @pl.when(inside(way, d))
            def _():
                pass_on(way, d).wait_send()
    w_y(own_part, 0, y_down).wait_send()
    w_y(own_part, 1, y_up).wait_send()
    w_core(own_part, 0).wait_send()
    w_core(far_part, 1).wait_send()
    for i in range(N_CHIP):
        to_partner(i).wait_send()
    for layer in range(2):
        for d in range(1, 4):
            to_owner(layer, lax.rem(y + d, 4)).wait_send()
    to_layer().wait_send()
    for copy in sent:
        copy.wait_send()
    for copy in outs:
        copy.wait()


def hand_over(*refs):
    count = len(refs) // 2
    for src, dst in zip(refs[:count], refs[count:]):
        dst[...] = src[...]


def per_device(q_in, k_in, v_in, log_decay, block_doc, w_out, grad_y):
    vmem = pl.BlockSpec(memory_space=pltpu.VMEM)
    hbm = pl.BlockSpec(memory_space=pl.ANY)
    dma = pltpu.SemaphoreType.DMA
    head_shape = jax.ShapeDtypeStruct((TOK, FEAT), BF16)
    shapes = (
        jax.ShapeDtypeStruct((TOK, COLS_Y), BF16),
        head_shape, head_shape, head_shape,
        jax.ShapeDtypeStruct((FEAT, COLS_W), BF16),
    )
    heads_vmem = pltpu.VMEM((TOK, FEAT), BF16)
    results = pl.pallas_call(
        kernel,
        out_shape=shapes,
        in_specs=[pl.BlockSpec(memory_space=pltpu.SMEM), vmem] + [hbm] * 5,
        out_specs=(hbm,) * 5,
        scratch_shapes=[
            heads_vmem, heads_vmem, heads_vmem,
            pltpu.VMEM((FEAT, D), BF16),
            pltpu.VMEM((TOK, D), BF16),
            heads_vmem, heads_vmem, heads_vmem,
            pltpu.VMEM((FEAT, COLS_W), BF16),
            pltpu.VMEM((TOK, COLS_Y), BF16),
            pltpu.VMEM((8, DH), F32),
            pltpu.VMEM((TOK, HEADS), F32),
            pltpu.VMEM((HEADS, TOK), F32),
            pltpu.VMEM((HEADS, DH, DH), F32),
            pltpu.VMEM((NBLK, HEADS, DH, DH), F32),
            pltpu.VMEM((NBLK, HEADS, DH, DH), BF16),
            pltpu.VMEM((NBLK, HEADS, DH, DH), F32),
            pltpu.VMEM((NBLK, HEADS, BL, BL), BF16),
            pltpu.VMEM((TOK, FEAT), F32),
            pltpu.VMEM((TOK, FEAT), F32),
            pltpu.VMEM((TOK, HEADS), F32),
            heads_vmem,
            pltpu.VMEM((FEAT, TOK), BF16),
            pltpu.VMEM((N_HEAD, TOK, FEAT), BF16),
            pltpu.VMEM((N_HEAD, W_PARTS, W_ROWS, COLS_Y), BF16),
            pltpu.VMEM((N_CHIP, FEAT, COLS_W), BF16),
            pltpu.VMEM((2, 4, FEAT, COLS_W), BF16),
            pltpu.VMEM((FEAT, COLS_W), BF16),
            pltpu.VMEM((2, FEAT, DH), BF16),
            pltpu.VMEM((2, FEAT, DH), BF16),
            pltpu.VMEM((2, FEAT // 2, DH), BF16),
            pltpu.VMEM((2, N_CHIP, FEAT // 2, DH), BF16),
            pltpu.VMEM((2, FEAT // 2, DH), BF16),
            pltpu.VMEM((2, FEAT // 2, DH), BF16),
            pltpu.VMEM((N_CTX, 8, DH), F32),
            pltpu.VMEM((2, 12, 8, DH), F32),
            pltpu.VMEM((HEADS, DH, DH), F32),
            pltpu.VMEM((TOK, COLS_Y), F32),
            dma((4 + 2 * (D // 1024),)), dma((5,)),
            dma((N_HEAD,)), dma((N_HEAD,)),
            dma((4,)), dma((4,)),
            dma((N_CTX,)), dma((N_CTX,)),
            dma((2, 2)), dma((2, 2)),
            dma((2, N_CHIP)), dma((2, N_CHIP)),
            dma((14,)), dma((N_HEAD, 2)),
            dma((N_CHIP,)), dma((N_CHIP,)),
            dma((2, 4)), dma((2, 4)),
            dma, dma,
        ],
        compiler_params=pltpu.CompilerParams(
            collective_id=0, has_side_effects=True, vmem_limit_bytes=63 << 20),
        name="attention_and_projection",
    )(block_doc, log_decay.T, q_in, k_in, v_in, w_out, grad_y)
    steps = 4
    specs = tuple(
        pl.BlockSpec((one.shape[0] // steps, one.shape[1]), lambda i: (i, 0)) for one in shapes)
    return pl.pallas_call(
        hand_over,
        out_shape=shapes,
        grid=(steps,),
        in_specs=specs,
        out_specs=specs,
        name="results",
    )(*results)


def solution(mesh):
    in_specs = (
        P("ctx", "head"),
        P("ctx", "head"),
        P("ctx", "head"),
        P("ctx", "head"),
        P("ctx"),
        P("head", None),
        P("ctx", None),
    )
    out_specs = (
        P("ctx", "head"),
        P("ctx", "head"),
        P("ctx", "head"),
        P("ctx", "head"),
        P("head", "ctx"),
    )
    return jax.shard_map(
        per_device, mesh=mesh, in_specs=in_specs, out_specs=out_specs, check_vma=False
    )
```

```python
import jax
import jax.numpy as jnp
from jax import lax
from jax.experimental import pallas as pl
from jax.experimental.pallas import tpu as pltpu
from jax.sharding import PartitionSpec as P

DH = 128
BL = 256
EPS = 1e-06
F32 = jnp.float32
BF16 = jnp.bfloat16
MESH = pl.DeviceIdType.MESH

N_CTX = 16
N_HEAD = 8
N_CHIP = 8
NBLK = 3
HEADS = 4
TOK = NBLK * BL
HALF = TOK // 2
FEAT = HEADS * DH
D = 6144
COLS_Y = D // N_HEAD
COLS_W = D // N_CTX
W_PARTS = 4
W_ROWS = FEAT // W_PARTS

NN = (((1,), (0,)), ((), ()))
NT = (((1,), (1,)), ((), ()))
TN = (((0,), (0,)), ((), ()))


def mm(a, b, dims=NN):
    return lax.dot_general(a, b, dims, preferred_element_type=F32)


def kernel(
    docs, ldt, q_hbm, k_hbm, v_hbm, w_hbm, gy_hbm,
    out_y_hbm, gq_hbm, gk_hbm, gv_hbm, gw_hbm,
    q, k, v, w, gy, gq, gk, gv, gw, out_y,
    scal, dsc, dsr, run, loc, sth, gloc, pr, att, gn, inv_s, ga, n_t,
    nall, wcol, crx, rs_rx, z_rx, sbuf, p_rx, cbuf, c_rx, ebuf, e_rx, scal_rx, wgt, entry, acc,
    lsem, osem, wa_s, wa_r, wg_s, wg_r, sc_s, sc_r, x_s, x_r, st_s, st_r,
    ag_s, ag_r, cs_s, cs_r, ps_s, ps_r, z_s, z_r,
):
    c = lax.axis_index("ctx")
    h = lax.axis_index("head")
    chip, core = c // 2, lax.rem(c, 2)
    partner = c + 1 - 2 * core
    zl, y = c // 8, lax.rem(chip, 4)
    y_up = zl * 8 + lax.rem(y + 1, 4) * 2 + core
    y_down = zl * 8 + lax.rem(y + 3, 4) * 2 + core
    z_peer = lax.rem(c + 8, N_CTX)
    own_part = lax.rem(y, 2) * 2 + core
    far_part = (1 - lax.rem(y, 2)) * 2 + core
    hx, hz = h // 2, lax.rem(h, 2)
    east = lax.rem(hx + 1, 4) * 2 + hz
    west = lax.rem(hx + 3, 4) * 2 + hz
    zp = hx * 2 + 1 - hz
    east_z = lax.rem(hx + 1, 4) * 2 + 1 - hz
    west_z = lax.rem(hx + 3, 4) * 2 + 1 - hz
    far = lax.rem(hx + 2, 4) * 2 + hz
    far_z = lax.rem(hx + 2, 4) * 2 + 1 - hz

    def remote(src, dst, ssem, rsem, to_c, to_h):
        return pltpu.make_async_remote_copy(
            src_ref=src, dst_ref=dst, send_sem=ssem, recv_sem=rsem,
            device_id=(to_c, to_h), device_id_type=MESH,
        )

    loads = [
        pltpu.make_async_copy(src, dst, lsem.at[i])
        for i, (src, dst) in enumerate(
            [(k_hbm, k), (v_hbm, v), (q_hbm, q)])
    ]
    step_k = 1024
    steps_k = D // step_k

    def load_columns(i):
        at = pl.ds(pl.multiple_of(i * step_k, step_k), step_k)
        return [
            pltpu.make_async_copy(w_hbm.at[:, at], w.at[:, at], lsem.at[4 + i]),
            pltpu.make_async_copy(gy_hbm.at[:, at], gy.at[:, at], lsem.at[4 + steps_k + i]),
        ]


    def w_piece(to):
        return w_hbm.at[pl.ds(pl.multiple_of(own_part * W_ROWS, W_ROWS), W_ROWS),
                        pl.ds(pl.multiple_of(to * COLS_Y, COLS_Y), COLS_Y)]

    own_w = pltpu.make_async_copy(w_piece(h), wcol.at[h, own_part], lsem.at[3])
    for copy in loads:
        copy.start()

    def w_peer(d):
        to_x, to_z = lax.rem(hx + d // 2, 4), lax.rem(hz + d % 2, 2)
        return (z_peer if d % 2 else c), to_x * 2 + to_z

    barrier = pltpu.get_barrier_semaphore()
    for d in range(1, N_HEAD, 2):
        pl.semaphore_signal(barrier, inc=1, device_id=w_peer(d), device_id_type=MESH)
    for d in range(1, N_CTX):
        pl.semaphore_signal(barrier, inc=1, device_id=(lax.rem(c + d, N_CTX), h),
                            device_id_type=MESH)
    for d in range(1, N_HEAD):
        pl.semaphore_signal(barrier, inc=1, device_id=(c, lax.rem(h + d, N_HEAD)),
                            device_id_type=MESH)
    pl.semaphore_wait(barrier, N_CTX + N_HEAD - 2 + N_HEAD // 2)

    def w_spread(d):
        to_c, to = w_peer(d)
        return remote(w_piece(to), wcol.at[h, own_part], wa_s.at[d], wa_r.at[h], to_c, to)

    def scal_spread(d):
        return remote(scal, scal_rx.at[c], sc_s.at[d], sc_r.at[c], lax.rem(c + d, N_CTX), h)

    own_w.start()
    for d in range(1, N_HEAD):
        w_spread(d).start()
    for i in range(steps_k):
        for copy in load_columns(i):
            copy.start()
    at_row = lax.broadcasted_iota(jnp.int32, (BL, BL), 0)
    at_col = lax.broadcasted_iota(jnp.int32, (BL, BL), 1)
    lower = at_row >= at_col

    def doc_row(b):
        return jnp.full((1, DH), docs[b], jnp.int32).astype(F32)

    keep1 = jnp.where(doc_row(0) == doc_row(1), 1.0, 0.0)
    keep2 = jnp.where(doc_row(1) == doc_row(2), 1.0, 0.0)

    def rows_of(b):
        return pl.ds(pl.multiple_of(b * BL, BL), BL)

    def cols_of(hh):
        return slice(hh * DH, (hh + 1) * DH)

    def mask_of(rows, hh):
        gap = dsc[rows, hh:hh + 1] - dsr[hh:hh + 1, rows]
        return jnp.where(lower, jnp.exp(jnp.minimum(gap, 0.0)), 0.0)

    def pick(b, zero, one, two):
        return jnp.where(b == 0, zero, jnp.where(b == 1, one, two))

    run[...] = jnp.zeros_like(run)

    tri = jnp.where(lower, 1.0, 0.0).astype(F32)
    exact = dict(precision=lax.Precision.HIGHEST, preferred_element_type=F32)

    def sums(b, carry):
        rows = rows_of(b)
        dsc[rows, :] = lax.dot_general(tri, ldt[:, rows], NT, **exact)
        dsr[:, rows] = lax.dot_general(ldt[:, rows], tri, NT, **exact)
        return carry

    lax.fori_loop(0, NBLK, sums, 0)
    ends = [dsr[:, (b + 1) * BL - 1:(b + 1) * BL] for b in range(NBLK)]
    scal[0:HEADS, :] = jnp.broadcast_to(ends[0] + ends[1] + ends[2], (HEADS, DH))
    for row, b in ((4, 0), (5, NBLK - 1), (6, 1), (7, 1)):
        scal[row:row + 1, :] = doc_row(b)
    for d in range(1, N_CTX):
        scal_spread(d).start()
    scal_rx[c] = scal[...]

    def local_states(b, carry):
        rows = rows_of(b)
        kept = pick(b, keep1, keep2, jnp.ones_like(keep1))
        for hh in range(HEADS):
            col = dsc[rows, hh:hh + 1]
            end = col[BL - 1:BL, :]
            kw = (k[rows, cols_of(hh)].astype(F32) * jnp.exp(end - col)).astype(BF16)
            update = mm(kw, v[rows, cols_of(hh)], TN)
            loc[b, hh] = run[hh]
            run[hh] = kept * (jnp.exp(end) * run[hh] + update)
        return carry

    loads[0].wait()
    loads[1].wait()
    lax.fori_loop(0, NBLK, local_states, 0)
    for hh in range(HEADS):
        sbuf[0, cols_of(hh), :] = run[hh].astype(BF16)

    def pair(way):
        return remote(sbuf.at[way], p_rx.at[way], x_s.at[way, 0], x_r.at[way, 0], partner, h)

    def pass_on(way, d):
        to = chip - d if way else chip + d
        return remote(cbuf.at[way], c_rx.at[way, chip], st_s.at[way, d], st_r.at[way, chip],
                      2 * to + core, h)

    def swap(way):
        return remote(ebuf.at[way], e_rx.at[way], x_s.at[way, 1], x_r.at[way, 1], partner, h)

    def inside(way, d):
        return (chip >= d) if way else (chip + d < N_CHIP)

    pair(0).start()

    def intra(b, carry):
        rows = rows_of(b)
        for hh in range(HEADS):
            cols = cols_of(hh)
            probs = (mm(q[rows, cols], k[rows, cols], NT) * mask_of(rows, hh)).astype(BF16)
            pr[b, hh] = probs
            att[rows, cols] = mm(probs, v[rows, cols])
        return carry

    loads[2].wait()
    lax.fori_loop(0, NBLK, intra, 0)

    for d in range(1, N_CTX):
        src = lax.rem(c + d, N_CTX)
        remote(scal, scal_rx.at[src], sc_s.at[d], sc_r.at[src], src, h).wait_recv()

    for way in range(2):
        total = jnp.zeros((8, DH), F32)
        mine = scal_rx[2 * chip + 1, 5:6, :] if way else scal_rx[2 * chip, 4:5, :]
        for r in range(N_CHIP) if way else range(N_CHIP - 1, -1, -1):
            theirs = scal_rx[2 * r, 4:5, :] if way else scal_rx[2 * r + 1, 5:6, :]
            here = jnp.where((r > chip) if way else (r < chip), 1.0, 0.0)
            wgt[way, r] = jnp.exp(total) * jnp.where(theirs == mine, here, 0.0)
            total = total + here * (scal_rx[2 * r] + scal_rx[2 * r + 1])

    one = jnp.ones((8, DH), F32)

    def same(row, other):
        return jnp.where(scal_rx[2 * chip, row:row + 1, :] == scal_rx[2 * chip + 1, other:other + 1, :],
                         1.0, 0.0)

    log0, log1 = scal_rx[2 * chip], scal_rx[2 * chip + 1]
    from_core0 = jnp.exp(log1) * same(5, 5)
    from_core1 = jnp.exp(log0) * same(4, 4)
    through0 = jnp.exp(log0) * same(4, 4)
    through1 = jnp.exp(log1) * same(5, 5)
    link = same(5, 4) * one
    is0 = core == 0
    wgt[0, 8] = jnp.where(is0, from_core0, one)
    wgt[0, 9] = jnp.where(is0, one, from_core0)
    wgt[0, 10] = jnp.where(is0, one, through0)
    wgt[0, 11] = jnp.where(is0, 0.0, link)
    wgt[1, 8] = jnp.where(is0, one, from_core1)
    wgt[1, 9] = jnp.where(is0, from_core1, one)
    wgt[1, 10] = jnp.where(is0, through1, one)
    wgt[1, 11] = jnp.where(is0, link, 0.0)

    def head_rows(j):
        return pl.ds(pl.multiple_of((2 * core + j) * DH, DH), DH)

    def chip_state(way):
        pair(way).wait_recv()
        for j in range(2):
            hh = 2 * core + j
            cbuf[way, cols_of(j), :] = (
                wgt[way, 8, pl.ds(hh, 1), :] * run[hh]
                + wgt[way, 9, pl.ds(hh, 1), :] * p_rx[way, head_rows(j), :].astype(F32)
            ).astype(BF16)
        for d in range(1, N_CHIP):
            @pl.when(inside(way, d))
            def _():
                pass_on(way, d).start()

    def chip_entry(way):
        ebuf_f = entry
        for j in range(2):
            ebuf_f[j] = jnp.zeros((DH, DH), F32)

        def add(r, carry):
            @pl.when((r > chip) if way else (r < chip))
            def _():
                remote(cbuf.at[way], c_rx.at[way, r], st_s.at[way, 0], st_r.at[way, r],
                       2 * r + core, h).wait_recv()
                for j in range(2):
                    ebuf_f[j] += (wgt[way, r, pl.ds(2 * core + j, 1), :]
                                  * c_rx[way, r, cols_of(j), :].astype(F32))
            return carry

        lax.fori_loop(0, N_CHIP, add, 0)
        for j in range(2):
            ebuf[way, cols_of(j), :] = ebuf_f[j].astype(BF16)
        swap(way).start()

    def own_entry(way):
        swap(way).wait_recv()
        for j in range(2):
            for hh, chips in ((2 * core + j, ebuf), (2 * (1 - core) + j, e_rx)):
                rows = pl.ds(pl.multiple_of(hh * DH, DH), DH)
                entry[hh] = (wgt[way, 10, pl.ds(hh, 1), :] * chips[way, cols_of(j), :].astype(F32)
                             + wgt[way, 11, pl.ds(hh, 1), :] * p_rx[way, rows, :].astype(F32))

    chip_state(0)


    gn[...] = jnp.zeros_like(gn)

    def grad_normed(i, carry):
        for copy in load_columns(i):
            copy.wait()
        at = pl.ds(pl.multiple_of(i * step_k, step_k), step_k)
        gn[...] += mm(gy[:, at], w[:, at], NT)
        return carry

    lax.fori_loop(0, 4, grad_normed, 0)
    chip_entry(0)
    lax.fori_loop(4, D // step_k, grad_normed, 0)
    own_entry(0)

    def end_of(b, hh):
        return jnp.exp(dsc[b * BL + BL - 1:(b + 1) * BL, hh:hh + 1])

    def inter(b, carry):
        rows = rows_of(b)
        for hh in range(HEADS):
            cols = cols_of(hh)
            coef1 = keep1 * end_of(0, hh)
            coef = pick(b, jnp.ones_like(keep1), coef1, keep2 * end_of(1, hh) * coef1)
            state = (loc[b, hh] + coef * entry[hh]).astype(BF16)
            sth[b, hh] = state
            a = att[rows, cols] + jnp.exp(dsc[rows, hh:hh + 1]) * mm(q[rows, cols], state)
            inv = lax.rsqrt(jnp.mean(a * a, axis=-1, keepdims=True) + EPS)
            n = a * inv
            att[rows, cols] = a
            inv_s[rows, hh:hh + 1] = inv
            nall[h, rows, cols] = n.astype(BF16)
            n_t[cols, rows] = n.T.astype(BF16)
        return carry

    lax.fori_loop(0, NBLK, inter, 0)

    def part(slot, half):
        return nall.at[slot, pl.ds(half * HALF, HALF), :]

    def hand(slot, half, sem, to):
        return remote(part(slot, half), part(slot, half), ag_s.at[sem], ag_r.at[slot, half], c, to)

    def arrive(slot, half):
        remote(part(slot, half), part(slot, half), ag_s.at[0], ag_r.at[slot, half], c, zp).wait_recv()

    sent = []

    def go(*args):
        copy = hand(*args)
        copy.start()
        sent.append(copy)

    for half in range(2):
        go(h, half, half, zp)
        go(h, half, 2 + half, east)
        go(h, half, 4 + half, west)

    run[...] = jnp.zeros_like(run)

    def local_grads(i, carry):
        b = NBLK - 1 - i
        rows = rows_of(b)
        kept = pick(b, jnp.ones_like(keep1), keep1, keep2)
        for hh in range(HEADS):
            cols = cols_of(hh)
            a, g, inv = att[rows, cols], gn[rows, cols], inv_s[rows, hh:hh + 1]
            mean = jnp.mean(g * a, axis=-1, keepdims=True)
            grad = (inv * (g - a * (inv * inv) * mean)).astype(BF16)
            ga[rows, cols] = grad
            col = dsc[rows, hh:hh + 1]
            qw = (q[rows, cols].astype(F32) * jnp.exp(col)).astype(BF16)
            direct = mm(qw, grad, TN)
            gloc[b, hh] = run[hh]
            run[hh] = kept * (direct + jnp.exp(col[BL - 1:BL, :]) * run[hh])
        return carry

    lax.fori_loop(0, NBLK, local_grads, 0)
    for hh in range(HEADS):
        sbuf[1, cols_of(hh), :] = run[hh].astype(BF16)

    pair(1).start()

    def w_cols(i, parity):
        return pl.ds(pl.multiple_of((2 * i + parity) * COLS_W, COLS_W), COLS_W)

    def to_partner(i):
        return remote(w.at[:, w_cols(i, 1 - core)], crx.at[i], cs_s.at[i], cs_r.at[i], partner, h)

    def from_partner(i):
        return remote(w.at[:, w_cols(i, core)], crx.at[i], cs_s.at[i], cs_r.at[i], partner, h)

    def order(j):
        return jnp.where(j < 4, 1 - zl, zl), lax.rem(y + 1 + lax.rem(j, 4), 4)

    def to_owner(layer, row):
        return remote(w.at[:, w_cols(layer * 4 + row, core)], rs_rx.at[layer, y],
                      ps_s.at[layer, row], ps_r.at[layer, y], zl * 8 + row * 2 + core, h)

    def columns(j, carry):
        layer, row = order(j)
        i = layer * 4 + row
        at = pl.ds(pl.multiple_of(i * 2 * COLS_W, 2 * COLS_W), 2 * COLS_W)
        w[:, at] = mm(n_t[...], gy[:, at]).astype(BF16)
        to_partner(i).start()
        return carry

    def chip_sum(j):
        layer, row = order(j)
        i = layer * 4 + row
        at = w_cols(i, core)
        from_partner(i).wait_recv()
        both = (w[:, at].astype(F32) + crx[i].astype(F32)).astype(BF16)

        @pl.when(lax.rem(j, 4) < 3)
        def _():
            w[:, at] = both
            to_owner(layer, row).start()

        @pl.when(lax.rem(j, 4) == 3)
        def _():
            rs_rx[layer, y] = both

    def columns_and_sum(j, carry):
        columns(j, carry)
        chip_sum(j - 2)
        return carry

    lax.fori_loop(0, 2, columns, 0)
    chip_state(1)

    own_w.wait()
    for d in range(1, N_HEAD):
        from_c, src = w_peer(d)
        remote(w_piece(h), wcol.at[src, own_part], wa_s.at[d], wa_r.at[src], from_c, src).wait_recv()

    def w_half(part, half):
        return wcol.at[:, part, pl.ds(half * (W_ROWS // 2), W_ROWS // 2)]

    def w_y(part, half, to):
        return remote(w_half(part, half), w_half(part, half), wg_s.at[half], wg_r.at[half], to, h)

    def w_core(part, i):
        return remote(wcol.at[:, part], wcol.at[:, part], wg_s.at[2 + i], wg_r.at[2 + i], partner, h)

    w_y(own_part, 0, y_down).start()
    w_y(own_part, 1, y_up).start()
    w_core(own_part, 0).start()

    lax.fori_loop(2, N_CHIP, columns_and_sum, 0)
    chip_sum(jnp.int32(N_CHIP - 2))
    chip_sum(jnp.int32(N_CHIP - 1))

    arrive(west, 0)
    go(west, 0, 6, east)
    arrive(east, 1)
    go(east, 1, 7, west)
    chip_entry(1)
    arrive(zp, 0)
    go(zp, 0, 8, east)
    go(zp, 0, 10, west)
    own_entry(1)

    def backward(b, carry):
        rows = rows_of(b)
        for hh in range(HEADS):
            cols = cols_of(hh)
            coef1 = keep2 * end_of(2, hh)
            coef = pick(b, keep1 * end_of(1, hh) * coef1, coef1, jnp.ones_like(keep1))
            sg = (gloc[b, hh] + coef * entry[hh]).astype(BF16)
            qb, kb, vb, gb = q[rows, cols], k[rows, cols], v[rows, cols], ga[rows, cols]
            col = dsc[rows, hh:hh + 1]
            tail = jnp.exp(col[BL - 1:BL, :] - col)
            ds = (mm(gb, vb, NT) * mask_of(rows, hh)).astype(BF16)
            gq[rows, cols] = (mm(ds, kb) + jnp.exp(col) * mm(gb, sth[b, hh], NT)).astype(BF16)
            gk[rows, cols] = (mm(ds, qb, TN) + tail * mm(vb, sg, NT)).astype(BF16)
            kw = (kb.astype(F32) * tail).astype(BF16)
            gv[rows, cols] = (mm(pr[b, hh], gb, TN) + mm(kw, sg)).astype(BF16)
        return carry

    lax.fori_loop(0, NBLK, backward, 0)

    arrive(zp, 1)
    go(zp, 1, 9, east)
    go(zp, 1, 11, west)
    for half in range(2):
        arrive(far, half)
        go(far, half, 12 + half, zp)

    w_y(far_part, 0, y_up).wait_recv()
    w_y(far_part, 1, y_down).wait_recv()
    w_core(far_part, 1).start()
    outs = [pltpu.make_async_copy(src, dst, osem.at[i]) for i, (src, dst) in enumerate(
        [(gq, gq_hbm), (gk, gk_hbm), (gv, gv_hbm), (gw, gw_hbm), (out_y, out_y_hbm)])]
    for copy in outs[:3]:
        copy.start()
    w_core(1 - core + 2 * lax.rem(y, 2), 0).wait_recv()
    w_core(1 - core + 2 * (1 - lax.rem(y, 2)), 1).wait_recv()

    def product(slot, start):
        def rows_step(b, carry):
            rows = rows_of(b)
            term = mm(nall[slot, rows, :], wcol[slot].reshape(FEAT, COLS_Y))
            if start:
                acc[rows, :] = term
            else:
                acc[rows, :] += term
            return carry

        lax.fori_loop(0, NBLK, rows_step, 0)

    product(h, True)
    arrive(west, 1)
    product(west, False)
    arrive(east, 0)
    product(east, False)
    product(zp, False)
    product(far, False)

    def from_row(layer, d):
        row = lax.rem(y + d, 4)
        remote(w.at[:, w_cols(layer * 4 + y, core)], rs_rx.at[layer, row], ps_s.at[layer, row],
               ps_r.at[layer, row], c, h).wait_recv()

    def along_y(layer):
        for d in range(1, 4):
            from_row(layer, d)
        return sum(rs_rx[layer, row].astype(F32) for row in range(4))

    def to_layer():
        return remote(rs_rx.at[1 - zl, y], z_rx, z_s, z_r, z_peer, h)

    rs_rx[1 - zl, y] = along_y(1 - zl).astype(BF16)
    to_layer().start()

    arrive(west_z, 0)
    arrive(west_z, 1)
    product(west_z, False)
    arrive(east_z, 0)
    arrive(east_z, 1)
    product(east_z, False)
    gw_mine = along_y(zl)
    to_layer().wait_recv()
    gw[...] = (gw_mine + z_rx[...].astype(F32)).astype(BF16)
    outs[3].start()
    arrive(far_z, 0)
    arrive(far_z, 1)
    product(far_z, False)
    out_y[...] = acc[...].astype(BF16)
    outs[4].start()

    for d in range(1, N_HEAD):
        w_spread(d).wait_send()
    for d in range(1, N_CTX):
        scal_spread(d).wait_send()
    for way in range(2):
        pair(way).wait_send()
        swap(way).wait_send()
        for d in range(1, N_CHIP):
            @pl.when(inside(way, d))
            def _():
                pass_on(way, d).wait_send()
    w_y(own_part, 0, y_down).wait_send()
    w_y(own_part, 1, y_up).wait_send()
    w_core(own_part, 0).wait_send()
    w_core(far_part, 1).wait_send()
    for i in range(N_CHIP):
        to_partner(i).wait_send()
    for layer in range(2):
        for d in range(1, 4):
            to_owner(layer, lax.rem(y + d, 4)).wait_send()
    to_layer().wait_send()
    for copy in sent:
        copy.wait_send()
    for copy in outs:
        copy.wait()


def hand_over(*refs):
    *arrays, in_sem, out_sem = refs
    count = len(arrays) // 3
    srcs, dsts, bufs = arrays[:count], arrays[count:2 * count], arrays[2 * count:]
    ins = [pltpu.make_async_copy(srcs[i], bufs[i], in_sem.at[i]) for i in range(count)]
    outs = [pltpu.make_async_copy(bufs[i], dsts[i], out_sem.at[i]) for i in range(count)]
    for copy in ins:
        copy.start()
    for i in range(count):
        ins[i].wait()
        outs[i].start()
    for copy in outs:
        copy.wait()


def per_device(q_in, k_in, v_in, log_decay, block_doc, w_out, grad_y):
    vmem = pl.BlockSpec(memory_space=pltpu.VMEM)
    hbm = pl.BlockSpec(memory_space=pl.ANY)
    dma = pltpu.SemaphoreType.DMA
    head_shape = jax.ShapeDtypeStruct((TOK, FEAT), BF16)
    shapes = (
        jax.ShapeDtypeStruct((TOK, COLS_Y), BF16),
        head_shape, head_shape, head_shape,
        jax.ShapeDtypeStruct((FEAT, COLS_W), BF16),
    )
    heads_vmem = pltpu.VMEM((TOK, FEAT), BF16)
    results = pl.pallas_call(
        kernel,
        out_shape=shapes,
        in_specs=[pl.BlockSpec(memory_space=pltpu.SMEM), vmem] + [hbm] * 5,
        out_specs=(hbm,) * 5,
        scratch_shapes=[
            heads_vmem, heads_vmem, heads_vmem,
            pltpu.VMEM((FEAT, D), BF16),
            pltpu.VMEM((TOK, D), BF16),
            heads_vmem, heads_vmem, heads_vmem,
            pltpu.VMEM((FEAT, COLS_W), BF16),
            pltpu.VMEM((TOK, COLS_Y), BF16),
            pltpu.VMEM((8, DH), F32),
            pltpu.VMEM((TOK, HEADS), F32),
            pltpu.VMEM((HEADS, TOK), F32),
            pltpu.VMEM((HEADS, DH, DH), F32),
            pltpu.VMEM((NBLK, HEADS, DH, DH), F32),
            pltpu.VMEM((NBLK, HEADS, DH, DH), BF16),
            pltpu.VMEM((NBLK, HEADS, DH, DH), F32),
            pltpu.VMEM((NBLK, HEADS, BL, BL), BF16),
            pltpu.VMEM((TOK, FEAT), F32),
            pltpu.VMEM((TOK, FEAT), F32),
            pltpu.VMEM((TOK, HEADS), F32),
            heads_vmem,
            pltpu.VMEM((FEAT, TOK), BF16),
            pltpu.VMEM((N_HEAD, TOK, FEAT), BF16),
            pltpu.VMEM((N_HEAD, W_PARTS, W_ROWS, COLS_Y), BF16),
            pltpu.VMEM((N_CHIP, FEAT, COLS_W), BF16),
            pltpu.VMEM((2, 4, FEAT, COLS_W), BF16),
            pltpu.VMEM((FEAT, COLS_W), BF16),
            pltpu.VMEM((2, FEAT, DH), BF16),
            pltpu.VMEM((2, FEAT, DH), BF16),
            pltpu.VMEM((2, FEAT // 2, DH), BF16),
            pltpu.VMEM((2, N_CHIP, FEAT // 2, DH), BF16),
            pltpu.VMEM((2, FEAT // 2, DH), BF16),
            pltpu.VMEM((2, FEAT // 2, DH), BF16),
            pltpu.VMEM((N_CTX, 8, DH), F32),
            pltpu.VMEM((2, 12, 8, DH), F32),
            pltpu.VMEM((HEADS, DH, DH), F32),
            pltpu.VMEM((TOK, COLS_Y), F32),
            dma((4 + 2 * (D // 1024),)), dma((5,)),
            dma((N_HEAD,)), dma((N_HEAD,)),
            dma((4,)), dma((4,)),
            dma((N_CTX,)), dma((N_CTX,)),
            dma((2, 2)), dma((2, 2)),
            dma((2, N_CHIP)), dma((2, N_CHIP)),
            dma((14,)), dma((N_HEAD, 2)),
            dma((N_CHIP,)), dma((N_CHIP,)),
            dma((2, 4)), dma((2, 4)),
            dma, dma,
        ],
        compiler_params=pltpu.CompilerParams(
            collective_id=0, has_side_effects=True, vmem_limit_bytes=63 << 20),
        name="attention_and_projection",
    )(block_doc, log_decay.T, q_in, k_in, v_in, w_out, grad_y)
    return pl.pallas_call(
        hand_over,
        out_shape=shapes,
        in_specs=[hbm] * 5,
        out_specs=(hbm,) * 5,
        scratch_shapes=[pltpu.VMEM(one.shape, BF16) for one in shapes] + [dma((5,)), dma((5,))],
        name="results",
    )(*results)


def solution(mesh):
    in_specs = (
        P("ctx", "head"),
        P("ctx", "head"),
        P("ctx", "head"),
        P("ctx", "head"),
        P("ctx"),
        P("head", None),
        P("ctx", None),
    )
    out_specs = (
        P("ctx", "head"),
        P("ctx", "head"),
        P("ctx", "head"),
        P("ctx", "head"),
        P("head", "ctx"),
    )
    return jax.shard_map(
        per_device, mesh=mesh, in_specs=in_specs, out_specs=out_specs, check_vma=False
    )
```
